32 devices in a mesh: rep: 4 (over x, core), shard: 8 (over z, y).
Axes of the slice: x: 2, y: 2, z: 4, core: 2. Of those that a mesh axis runs over, the one named last changes fastest.
Arguments:
- tokens: bfloat16 [8192, 1536], P(('rep', 'shard')), may hold values from -6 to 6
- cotangent: bfloat16 [8192, 1536], P(('rep', 'shard')), may hold values from -6 to 6
- segment: int32 [8192], P(('rep', 'shard')), may hold values from 0 to 3, as said below
- live_rows: int32 [32], P(('rep', 'shard')), may hold values from 256 to 256, as said below
- in_weight: float32 [1536, 6448], P('shard'), may hold values from -0.15625 to 0.15625
- out_weight: float32 [3072, 1536], P('shard'), may hold values from -0.109375 to 0.109375
- conv_table: float32 [5, 3328], P(None, 'shard'), may hold values from -0.5 to 0.5
- norm_in: float32 [1536], P('shard'), may hold values from 0.5 to 1.5
- norm_gate: float32 [3072], P('shard'), may hold values from 0.5 to 1.5
- head_params: float32 [3, 48], replicated, may hold values from -10 to 3, as said below
- in_first: float32 [1536, 6448], P('shard'), may hold values from -18 to 18
- out_first: float32 [3072, 1536], P('shard'), may hold values from -18 to 18
- conv_first: float32 [5, 3328], P(None, 'shard'), may hold values from -18 to 18
- norm_in_first: float32 [1536], P('shard'), may hold values from -18 to 18
- norm_gate_first: float32 [3072], P('shard'), may hold values from -18 to 18
- heads_first: float32 [3, 48], replicated, may hold values from -18 to 18
- in_second: float32 [1536, 6448], P('shard'), may hold values from 1 to 1000
- out_second: float32 [3072, 1536], P('shard'), may hold values from 1 to 1000
- conv_second: float32 [5, 3328], P(None, 'shard'), may hold values from 1 to 1000
- norm_in_second: float32 [1536], P('shard'), may hold values from 1 to 1000
- norm_gate_second: float32 [3072], P('shard'), may hold values from 1 to 1000
- heads_second: float32 [3, 48], replicated, may hold values from 1 to 1000
Outputs:
- block_out: bfloat16 [8192, 1536], P(('rep', 'shard'))
- input_grad: bfloat16 [8192, 1536], P(('rep', 'shard'))
- grad_in_weight: float32 [1536, 6448], P('shard')
- grad_out_weight: float32 [3072, 1536], P('shard')
- grad_conv: float32 [5, 3328], P(None, 'shard')
- grad_norm_in: float32 [1536], P('shard')
- grad_norm_gate: float32 [3072], P('shard')
- grad_heads: float32 [3, 48], replicated
- new_in_weight: float32 [1536, 6448], P('shard')
- new_out_weight: float32 [3072, 1536], P('shard')
- new_conv: float32 [5, 3328], P(None, 'shard')
- new_norm_in: float32 [1536], P('shard')
- new_norm_gate: float32 [3072], P('shard')
- new_heads: float32 [3, 48], replicated
- new_in_first: float32 [1536, 6448], P('shard')
- new_out_first: float32 [3072, 1536], P('shard')
- new_conv_first: float32 [5, 3328], P(None, 'shard')
- new_norm_in_first: float32 [1536], P('shard')
- new_norm_gate_first: float32 [3072], P('shard')
- new_heads_first: float32 [3, 48], replicated
- new_in_second: float32 [1536, 6448], P('shard')
- new_out_second: float32 [3072, 1536], P('shard')
- new_conv_second: float32 [5, 3328], P(None, 'shard')
- new_norm_in_second: float32 [1536], P('shard')
- new_norm_gate_second: float32 [3072], P('shard')
- new_heads_second: float32 [3, 48], replicated
The draws below stay inside these ranges and needn't reach their ends.
Inputs may be any that keep to these rules, and one draw needn't show every extreme that they name: Within each group of 256 rows, segment numbers start at 0 and rise by 0 or 1 from one row to the next; some group reaches the largest number in every draw. `live_rows`: each entry is a multiple of 256; some group is full in every draw. `head_params`: row 0 holds log decay rates, row 1 skip gains, row 2 step biases.
All inputs are finite; a program needn't handle non-finite values.
Results may differ from the reference program's by a relative error of at most 0.012.
Values may be sent and summed in bfloat16 or wider, within the bound.
No kernel may reach another device: no remote copies, remote signals or barrier semaphores. Data moves between devices by JAX's collectives and lax.ppermute only.
A program may use at most 448 MiB of HBM per device.

```python
import math
import jax
import jax.numpy as jnp
from jax import lax

D = 1536
H = 48
KW = 4
SPAN = 256
CAP = 256
STEP = 3
INNER = 3072
CONV_CH = 3328
PROJ = 6448
TOKENS = 8192


def draw_segment(key, part):
    groups = TOKENS // CAP
    key_marks, key_group = jax.random.split(key)
    start_marks = jax.random.randint(key_marks, (groups, CAP), 0, CAP) < 3
    start_marks = start_marks.at[:, 0].set(True)
    chosen = jax.random.randint(key_group, (), 0, groups)
    spacing = CAP // 4
    forced = jnp.arange(CAP) % spacing == 0
    row_pick = (jnp.arange(groups) == chosen)[:, None] & forced[None, :]
    start_marks = start_marks | row_pick
    numbers = jnp.cumsum(start_marks.astype(jnp.int32), axis=1) - 1
    numbers = jnp.minimum(numbers, 3)
    return numbers.reshape(groups * CAP).astype(jnp.int32)


def draw_live_rows(key, part):
    groups = TOKENS // CAP
    key_count, key_full = jax.random.split(key)
    blocks = jax.random.randint(key_count, (groups,), 1, CAP // SPAN + 1)
    full_group = jax.random.randint(key_full, (), 0, groups)
    blocks = blocks.at[full_group].set(CAP // SPAN)
    return (blocks * SPAN).astype(jnp.int32)


def draw_head_params(key, part):
    key_rate, key_skip, key_step = jax.random.split(key, 3)
    step_low = math.log(0.001)
    step_high = math.log(0.1)
    rate_high = 16.0
    rate_logs = jnp.log(jax.random.uniform(key_rate, (H,), jnp.float32, 1.0, rate_high))
    skip_gain = jax.random.uniform(key_skip, (H,), jnp.float32, 0.5, 1.5)
    step_size = jnp.exp(jax.random.uniform(key_step, (H,), jnp.float32, step_low, step_high))
    step_bias = step_size + jnp.log(-jnp.expm1(-step_size))
    return jnp.stack([rate_logs, skip_gain, step_bias]).astype(jnp.float32)


def levels(stream_key, dims, pieces, low, top_value):
    level, own = 1.0, jax.random.fold_in(stream_key, 6)
    for dim, blocks in pieces:
        steps = jnp.exp(jax.random.uniform(jax.random.fold_in(own, dim), (blocks,), jnp.float32, low / len(pieces), top_value / len(pieces)))
        level = level * jnp.repeat(steps, dims[dim] // blocks).reshape([-1 if axis == dim else 1 for axis in range(len(dims))])
    return level


def scatter_about(stream_key, dims, scale, bound, cuts=(), held_as=jnp.bfloat16):
    factor_of = levels(stream_key, dims, cuts, -0.22, 0.18) if cuts else 1.0
    result = jax.random.normal(stream_key, dims, jnp.float32) * scale * factor_of
    return jnp.minimum(jnp.maximum(result, -bound), bound).astype(held_as)


def setup_inputs(seed: int = 0) -> dict:
    key_list = jax.random.split(jax.random.key(seed), 23)
    return {
        "tokens": scatter_about(key_list[0], (TOKENS, D), 1.0, 6.0, ((0, 32),)),
        "cotangent": scatter_about(key_list[1], (TOKENS, D), 1.0, 6.0, ((0, 32),)),
        "segment": draw_segment(jax.random.fold_in(key_list[22], 71), 0),
        "live_rows": draw_live_rows(jax.random.fold_in(key_list[22], 71), 0),
        "in_weight": scatter_about(key_list[4], (D, PROJ), D ** -0.5, 0.15625, ((0, 8),), jnp.float32),
        "out_weight": scatter_about(key_list[5], (INNER, D), INNER ** -0.5, 0.109375, ((0, 8),), jnp.float32),
        "conv_table": jnp.clip(jax.random.uniform(key_list[6], (KW + 1, CONV_CH), jnp.float32, -0.5, 0.5) * levels(key_list[6], (KW + 1, CONV_CH), ((1, 8),), -0.4, 0.0), -0.5, 0.5),
        "norm_in": jnp.clip(1.0 + 0.1 * jax.random.normal(key_list[7], (D,), jnp.float32), 0.5, 1.5),
        "norm_gate": jnp.clip(1.0 + 0.1 * jax.random.normal(key_list[8], (INNER,), jnp.float32), 0.5, 1.5),
        "head_params": draw_head_params(jax.random.fold_in(key_list[22], 71), 0),
        "in_first": scatter_about(key_list[10], (D, PROJ), 3.0, 18.0, ((0, 8),), jnp.float32),
        "out_first": scatter_about(key_list[11], (INNER, D), 3.0, 18.0, ((0, 8),), jnp.float32),
        "conv_first": scatter_about(key_list[12], (KW + 1, CONV_CH), 3.0, 18.0, ((1, 8),), jnp.float32),
        "norm_in_first": scatter_about(key_list[13], (D,), 3.0, 18.0, ((0, 8),), jnp.float32),
        "norm_gate_first": scatter_about(key_list[14], (INNER,), 3.0, 18.0, ((0, 8),), jnp.float32),
        "heads_first": scatter_about(key_list[15], (3, H), 3.0, 18.0, (), jnp.float32),
        "in_second": jnp.clip(jnp.exp(math.log(1000.0) - 6.9077553 * jax.random.uniform(key_list[16], (D, PROJ), jnp.float32) ** levels(key_list[16], (D, PROJ), ((0, 8),), -0.2, 0.2)), 1.0, 1000.0),
        "out_second": jnp.clip(jnp.exp(math.log(1000.0) - 6.9077553 * jax.random.uniform(key_list[17], (INNER, D), jnp.float32) ** levels(key_list[17], (INNER, D), ((0, 8),), -0.2, 0.2)), 1.0, 1000.0),
        "conv_second": jnp.clip(jnp.exp(math.log(1000.0) - 6.9077553 * jax.random.uniform(key_list[18], (KW + 1, CONV_CH), jnp.float32) ** levels(key_list[18], (KW + 1, CONV_CH), ((1, 8),), -0.2, 0.2)), 1.0, 1000.0),
        "norm_in_second": jnp.clip(jnp.exp(math.log(1000.0) - 6.9077553 * jax.random.uniform(key_list[19], (D,), jnp.float32) ** levels(key_list[19], (D,), ((0, 8),), -0.2, 0.2)), 1.0, 1000.0),
        "norm_gate_second": jnp.clip(jnp.exp(math.log(1000.0) - 6.9077553 * jax.random.uniform(key_list[20], (INNER,), jnp.float32) ** levels(key_list[20], (INNER,), ((0, 8),), -0.2, 0.2)), 1.0, 1000.0),
        "heads_second": jnp.clip(jnp.exp(jax.random.uniform(key_list[21], (3, H), jnp.float32, math.log(1.0), math.log(1000.0))), 1.0, 1000.0),
    }


norm_eps = 1e-05
beta_first = 0.9
beta_second = 0.95
adam_eps = 1e-08
weight_decay = 0.1
matrix_rate = 0.005
vector_rate = 0.05
highest = lax.Precision.HIGHEST

def pre_norm(values, gain_vector):
    return values * lax.rsqrt(lax.optimization_barrier(jnp.mean(values * values, axis=1, keepdims=True)) + norm_eps) * gain_vector

def mixer_core(projected, conv_tail, ssm_state, conv_table, head_params, gate_gain, segments_now, tail_segments, state_segment):
    block_rows = projected.shape[0]
    inner_width = gate_gain.shape[0]
    head_count = head_params.shape[1]
    head_size = inner_width // head_count
    conv_taps = conv_table.shape[0] - 1
    channels = conv_table.shape[1]
    state_size = (channels - inner_width) // 2
    gate_part = projected[:, :inner_width]
    conv_input = projected[:, inner_width:inner_width + channels]
    step_raw = projected[:, inner_width + channels:]
    extended = jnp.concatenate([conv_tail, conv_input], axis=0)
    extended_segments = jnp.concatenate([tail_segments, segments_now], axis=0)
    conv_sum = jnp.broadcast_to(conv_table[conv_taps], (block_rows, channels))
    for lag_index in range(conv_taps):
        offset = conv_taps - 1 - lag_index
        shifted = extended[offset:offset + block_rows]
        same_doc = extended_segments[offset:offset + block_rows] == segments_now
        conv_sum = conv_sum + jnp.where(same_doc[:, None], shifted, 0.0) * conv_table[lag_index]
    activated = jax.nn.silu(conv_sum)
    inputs_x = activated[:, :inner_width].reshape(block_rows, head_count, head_size)
    input_bmat = activated[:, inner_width:inner_width + state_size]
    output_cmat = activated[:, inner_width + state_size:]
    step_size = jax.nn.softplus(step_raw + head_params[2])
    log_decay = step_size * -jnp.exp(head_params[0])
    cumulative = jnp.cumsum(log_decay, axis=0)
    gram_matrix = jnp.dot(output_cmat, input_bmat.T, precision=highest)
    position = jnp.arange(block_rows)
    causal = (position[:, None] >= position[None, :]) & (segments_now[:, None] == segments_now[None, :])
    cum_heads = cumulative.T
    differences = jnp.where(causal[None], cum_heads[:, :, None] - cum_heads[:, None, :], 0.0)
    mixing = jnp.where(causal[None], jnp.exp(differences), 0.0) * gram_matrix[None]
    scaled_x = inputs_x * step_size[:, :, None]
    within = jnp.einsum('hij,jhp->hip', mixing, scaled_x, precision=highest)
    carried_in = jnp.exp(cumulative) * (segments_now == state_segment)[:, None]
    from_state = jnp.einsum('in,hpn->hip', output_cmat, ssm_state, precision=highest)
    mixer_sum = within + from_state * carried_in.T[:, :, None]
    mixer_sum = mixer_sum.transpose(1, 0, 2) + head_params[1][None, :, None] * inputs_x
    last_segment = segments_now[block_rows - 1]
    to_end = jnp.exp(cumulative[block_rows - 1][None, :] - cumulative) * (segments_now == last_segment)[:, None]
    new_state = ssm_state * (jnp.exp(cumulative[block_rows - 1]) * (state_segment == last_segment))[:, None, None]
    weighted_x = scaled_x * to_end[:, :, None]
    new_state = new_state + jnp.einsum('jhp,jn->hpn', weighted_x, input_bmat, precision=highest)
    gated = mixer_sum.reshape(block_rows, inner_width) * jax.nn.silu(gate_part)
    normed = gated * lax.rsqrt(lax.optimization_barrier(jnp.mean(gated * gated, axis=1, keepdims=True)) + norm_eps) * gate_gain
    return (normed, conv_input[block_rows - conv_taps + 1:], new_state)

def contract_rows(left_side, right_side):
    return lax.dot_general(left_side, right_side, (((0,), (0,)), ((), ())), preferred_element_type=jnp.float32)

def contract_cols(left_side, right_side):
    return lax.dot_general(left_side, right_side, (((1,), (1,)), ((), ())), preferred_element_type=jnp.float32)

def device_pass(tokens, cotangent, segment, live_rows, in_copy, out_copy, conv_copy, gain_in, gain_gate, head_params):
    tail_rows = KW - 1
    channels = conv_copy.shape[1]
    inner_width = gain_gate.shape[0]
    head_count = head_params.shape[1]
    head_size = inner_width // head_count
    state_size = (channels - inner_width) // 2
    blocks = tokens.shape[0] // SPAN
    live_blocks = live_rows // SPAN

    def slice_rows(source, block_index):
        return lax.dynamic_slice_in_dim(source, block_index * SPAN, SPAN, 0)

    def forward_step(block_index, loop_state):
        conv_tail, tail_segments, ssm_state, state_segment, outputs, saved_states, saved_tails, saved_marks, saved_segments = loop_state
        values = slice_rows(tokens, block_index).astype(jnp.float32)
        segments_now = slice_rows(segment, block_index)
        saved_states = saved_states.at[block_index].set(ssm_state)
        saved_tails = saved_tails.at[block_index].set(conv_tail)
        saved_marks = saved_marks.at[block_index].set(tail_segments)
        saved_segments = saved_segments.at[block_index].set(state_segment)
        inputs_half = pre_norm(values, gain_in).astype(jnp.bfloat16)
        projected = jnp.dot(inputs_half, in_copy, preferred_element_type=jnp.float32)
        mixer_out, new_tail, new_state = mixer_core(projected, conv_tail, ssm_state, conv_copy, head_params, gain_gate, segments_now, tail_segments, state_segment)
        branch = jnp.dot(mixer_out.astype(jnp.bfloat16), out_copy, preferred_element_type=jnp.float32)
        outputs = lax.dynamic_update_slice_in_dim(outputs, (values + branch).astype(jnp.bfloat16), block_index * SPAN, 0)
        return (new_tail, segments_now[SPAN - tail_rows:], new_state, segments_now[SPAN - 1], outputs, saved_states, saved_tails, saved_marks, saved_segments)
    start_state = (jnp.zeros((tail_rows, channels), jnp.float32), jnp.full((tail_rows,), -1, jnp.int32), jnp.zeros((head_count, head_size, state_size), jnp.float32), jnp.int32(-1), jnp.zeros(tokens.shape, jnp.bfloat16), jnp.zeros((blocks, head_count, head_size, state_size), jnp.float32), jnp.zeros((blocks, tail_rows, channels), jnp.float32), jnp.full((blocks, tail_rows), -1, jnp.int32), jnp.full((blocks,), -1, jnp.int32))
    forward_done = lax.fori_loop(0, live_blocks, forward_step, start_state)
    outputs, saved_states, saved_tails, saved_marks, saved_segments = forward_done[4:]

    def backward_step(step_index, loop_state):
        grad_tail, grad_state, grad_in, grad_out, grad_conv, grad_gain_in, grad_gain_gate, grad_heads, input_grad = loop_state
        block_index = live_blocks - 1 - step_index
        values = slice_rows(tokens, block_index).astype(jnp.float32)
        cot_rows = slice_rows(cotangent, block_index)
        segments_now = slice_rows(segment, block_index)
        normed, norm_pull = jax.vjp(pre_norm, values, gain_in)
        inputs_half = normed.astype(jnp.bfloat16)
        projected = jnp.dot(inputs_half, in_copy, preferred_element_type=jnp.float32)

        def core_local(projected_in, tail_in, state_in, conv_in, heads_in, gate_in):
            return mixer_core(projected_in, tail_in, state_in, conv_in, heads_in, gate_in, segments_now, saved_marks[block_index], saved_segments[block_index])
        primal_out, core_pull = jax.vjp(core_local, projected, saved_tails[block_index], saved_states[block_index], conv_copy, head_params, gain_gate)
        mixer_half = primal_out[0].astype(jnp.bfloat16)
        grad_mixer = contract_cols(cot_rows, out_copy)
        grad_projected, grad_tail_in, grad_state_in, conv_part, heads_part, gate_part = core_pull((grad_mixer, grad_tail, grad_state))
        projected_half = grad_projected.astype(jnp.bfloat16)
        grad_normed = contract_cols(projected_half, in_copy)
        grad_values, gain_part = norm_pull(grad_normed)
        rows_grad = (cot_rows.astype(jnp.float32) + grad_values).astype(jnp.bfloat16)
        input_grad = lax.dynamic_update_slice_in_dim(input_grad, rows_grad, block_index * SPAN, 0)
        grad_in = grad_in + contract_rows(inputs_half, projected_half)
        grad_out = grad_out + contract_rows(mixer_half, cot_rows)
        return (grad_tail_in, grad_state_in, grad_in, grad_out, grad_conv + conv_part, grad_gain_in + gain_part, grad_gain_gate + gate_part, grad_heads + heads_part, input_grad)
    back_start = (jnp.zeros((tail_rows, channels), jnp.float32), jnp.zeros((head_count, head_size, state_size), jnp.float32), jnp.zeros(in_copy.shape, jnp.float32), jnp.zeros(out_copy.shape, jnp.float32), jnp.zeros(conv_copy.shape, jnp.float32), jnp.zeros(gain_in.shape, jnp.float32), jnp.zeros(gain_gate.shape, jnp.float32), jnp.zeros(head_params.shape, jnp.float32), jnp.zeros(tokens.shape, jnp.bfloat16))
    back_done = lax.fori_loop(0, live_blocks, backward_step, back_start)
    return (outputs, back_done[8], back_done[2], back_done[3], back_done[4], back_done[5], back_done[6], back_done[7])

def adam_update(weight, first, second, gradient, rate):
    first_new = beta_first * first + (1.0 - beta_first) * gradient
    second_new = beta_second * second + (1.0 - beta_second) * gradient * gradient
    first_hat = first_new / (1.0 - beta_first ** STEP)
    second_hat = second_new / (1.0 - beta_second ** STEP)
    weight_new = weight - rate * (first_hat / (jnp.sqrt(second_hat) + adam_eps) + weight_decay * weight)
    return (weight_new, first_new, second_new)

def reference(tokens, cotangent, segment, live_rows, in_weight, out_weight, conv_table, norm_in, norm_gate, head_params, in_first, out_first, conv_first, norm_in_first, norm_gate_first, heads_first, in_second, out_second, conv_second, norm_in_second, norm_gate_second, heads_second):
    in_copy = in_weight.astype(jnp.bfloat16)
    out_copy = out_weight.astype(jnp.bfloat16)
    conv_copy = lax.optimization_barrier(conv_table.astype(jnp.bfloat16)).astype(jnp.float32)
    gain_in = lax.optimization_barrier(norm_in.astype(jnp.bfloat16)).astype(jnp.float32)
    gain_gate = lax.optimization_barrier(norm_gate.astype(jnp.bfloat16)).astype(jnp.float32)
    groups = live_rows.shape[0]
    width = tokens.shape[1]
    stacked = (tokens.reshape(groups, CAP, width), cotangent.reshape(groups, CAP, width), segment.reshape(groups, CAP), live_rows)
    start_sums = (jnp.zeros(in_weight.shape, jnp.float32), jnp.zeros(out_weight.shape, jnp.float32), jnp.zeros(conv_table.shape, jnp.float32), jnp.zeros(norm_in.shape, jnp.float32), jnp.zeros(norm_gate.shape, jnp.float32), jnp.zeros(head_params.shape, jnp.float32))

    def per_group(sums, item):
        group_tokens, group_cot, group_segment, group_live = item
        results = device_pass(group_tokens, group_cot, group_segment, group_live, in_copy, out_copy, conv_copy, gain_in, gain_gate, head_params)
        sums = tuple((total + piece for total, piece in zip(sums, results[2:])))
        return (sums, (results[0], results[1]))
    sums, (block_groups, grad_groups) = lax.scan(per_group, start_sums, stacked)
    grad_in_weight, grad_out_weight, grad_conv, grad_norm_in, grad_norm_gate, grad_heads = sums
    new_in = adam_update(in_weight, in_first, in_second, grad_in_weight, matrix_rate)
    new_out = adam_update(out_weight, out_first, out_second, grad_out_weight, matrix_rate)
    new_conv = adam_update(conv_table, conv_first, conv_second, grad_conv, vector_rate)
    new_gin = adam_update(norm_in, norm_in_first, norm_in_second, grad_norm_in, vector_rate)
    new_ggate = adam_update(norm_gate, norm_gate_first, norm_gate_second, grad_norm_gate, vector_rate)
    new_heads = adam_update(head_params, heads_first, heads_second, grad_heads, vector_rate)
    return (block_groups.reshape(tokens.shape), grad_groups.reshape(tokens.shape), grad_in_weight, grad_out_weight, grad_conv, grad_norm_in, grad_norm_gate, grad_heads, new_in[0], new_out[0], new_conv[0], new_gin[0], new_ggate[0], new_heads[0], new_in[1], new_out[1], new_conv[1], new_gin[1], new_ggate[1], new_heads[1], new_in[2], new_out[2], new_conv[2], new_gin[2], new_ggate[2], new_heads[2])
```

```python
import functools

import jax
import jax.numpy as jnp
from jax import lax
from jax.experimental import pallas as pl
from jax.experimental.pallas import tpu as pltpu
from jax.sharding import PartitionSpec as P

STEP = 3
norm_eps = 1e-05
beta_first = 0.9
beta_second = 0.95
adam_eps = 1e-08
weight_decay = 0.1
matrix_rate = 0.005
vector_rate = 0.05
highest = lax.Precision.HIGHEST
f32 = jnp.float32
bf16 = jnp.bfloat16
LANES = 128


def dot(a, b, contract, precision=None):
    return lax.dot_general(
        a, b, (((contract[0],), (contract[1],)), ((), ())),
        preferred_element_type=f32, precision=precision,
    )


def fence(value, *after):
    return lax.optimization_barrier((value, *after))[0]


def rep_swap(x, bit, reps):
    return lax.ppermute(x, "rep", [(i, i ^ bit) for i in range(reps)])


def rep_bits(reps):
    return [1 << k for k in reversed(range(reps.bit_length() - 1))]


def rep_gather(x, reps):
    have = {0: x}
    for bit in rep_bits(reps):
        have.update({j | bit: rep_swap(v, bit, reps) for j, v in list(have.items())})
    return [have[j] for j in range(reps)]


def rep_scatter_sum(blocks, reps, wire):
    have = {j: b for j, b in enumerate(blocks)}
    for bit in reversed(rep_bits(reps)):
        keep = [j for j in have if not j & bit]
        have = {
            j: have[j].astype(f32) + rep_swap(have[j | bit].astype(wire), bit, reps).astype(f32)
            for j in keep
        }
    return have[0]


def line(count, step, first, last):
    return [
        (2 * z + y, 2 * (z + step) + y) for z in range(first, last + 1) for y in range(2) if 0 <= z + step < count
    ]


def gather_shards(block, shards):
    rows, columns = block.shape
    depth = shards // 2
    if shards % 2 or depth > 4 or depth < 2:
        return lax.all_gather(block, "shard", axis=0, tiled=True)
    me = lax.axis_index("shard")
    z, y = me // 2, me % 2

    def across(value, zs):
        return lax.ppermute(value, "shard", [(2 * k + i, 2 * k + 1 - i) for k in zs for i in range(2)])

    near = {0: [block]}
    far = {0: [across(block, range(depth))]}
    up = down = block
    for k in range(1, depth):
        up = lax.ppermute(up, "shard", line(depth, 1, k - 1, depth - 2))
        down = lax.ppermute(down, "shard", line(depth, -1, 1, depth - k))
        near.setdefault(depth - k, []).append(up)
        near.setdefault(k, []).append(down)
        far.setdefault(depth - k, []).append(across(up, range(k, depth)))
        far.setdefault(k, []).append(across(down, range(0, depth - k)))
    full = jnp.zeros((shards, rows, columns), block.dtype)
    for j in range(depth):
        for side, parts in ((y, near[j]), (1 - y, far[j])):
            value = functools.reduce(jnp.add, parts)
            full = lax.dynamic_update_slice(full, value[None], (2 * ((z + j) % depth) + side, 0, 0))
    return full.reshape(shards * rows, columns)


def reduce_shards(parts, shards):
    depth = shards // 2
    if shards % 2 or depth > 4 or depth < 2:
        return lax.psum_scatter(parts, "shard", scatter_dimension=0, tiled=True)[0].astype(f32)
    me = lax.axis_index("shard")
    z, y = me // 2, me % 2
    swap = [(i, i ^ 1) for i in range(shards)]

    def block(j, side):
        return lax.dynamic_index_in_dim(parts, 2 * ((z + j) % depth) + side, 0, keepdims=False)

    order = []
    for k in range(depth - 1, 0, -1):
        order += [j for j in (k, depth - k) if j not in order]
    order.append(0)
    sums = {}
    for j in order:
        sums[j] = block(j, y).astype(f32) + lax.ppermute(block(j, 1 - y), "shard", swap).astype(f32)
    up = down = None
    for k in range(depth - 1, 0, -1):
        send_up = sums[k] if up is None else sums[k] + up
        send_down = sums[depth - k] if down is None else sums[depth - k] + down
        up = lax.ppermute(send_up.astype(bf16), "shard", line(depth, 1, 0, depth - 1 - k)).astype(f32)
        down = lax.ppermute(send_down.astype(bf16), "shard", line(depth, -1, k, depth - 1)).astype(f32)
    return sums[0] + up + down


def sum_shards(x, shards):
    if shards & (shards - 1):
        return lax.psum(x, "shard")
    bit = 1
    while bit < shards:
        x = x + lax.ppermute(x, "shard", [(i, i ^ bit) for i in range(shards)])
        bit *= 2
    return x


def softplus(v):
    return jnp.maximum(v, 0.0) + jnp.log1p(jnp.exp(-jnp.abs(v)))


def sigmoid(v):
    return 1.0 / (1.0 + jnp.exp(-v))


def iota(shape, axis):
    return lax.broadcasted_iota(jnp.int32, shape, axis)


def conv_piece(raw, meta, conv_ref, lanes, taps):
    total = conv_ref[taps : taps + 1, lanes] + conv_ref[0:1, lanes] * raw
    for k in range(1, taps):
        total = total + conv_ref[k : k + 1, lanes] * (meta[:, k : k + 1] * pltpu.roll(raw, k, 0))
    return total


def rates(raw, heads_ref):
    span = raw.shape[0]
    pre = raw + heads_ref[1:2, :]
    step = softplus(pre)
    log_decay = step * heads_ref[0:1, :]
    lower = (iota((span, span), 0) >= iota((span, span), 1)).astype(f32)
    running = dot(lower, log_decay, (1, 0), highest)
    return pre, step, log_decay, running, running.T


def spread(columns, first, count, head_size):
    lane = iota((columns.shape[0], LANES), 1) // head_size
    value = jnp.broadcast_to(columns[:, first : first + 1], lane.shape)
    for k in range(1, count):
        value = jnp.where(lane == k, columns[:, first + k : first + k + 1], value)
    return value


def forward_kernel(u_ref, w_ref, conv_ref, heads_ref, skip_ref, meta_ref, row_ref, p_ref, y_ref, act_ref, *, dims):
    hc, state, hs, taps = dims
    span = u_ref.shape[0]
    wide = hc + 2 * state
    p_ref[...] = jnp.dot(u_ref[...], w_ref[...], preferred_element_type=f32)
    meta = meta_ref[...]
    for c in range(0, wide, 2 * LANES):
        lanes = pl.ds(c, min(2 * LANES, wide - c))
        conv = conv_piece(p_ref[:, lanes], meta, conv_ref, lanes, taps)
        act_ref[:, lanes] = conv * sigmoid(conv)
    _, step, _, running, running_t = rates(p_ref[:, wide : wide + LANES], heads_ref)
    gram = dot(act_ref[:, hc + state : wide], act_ref[:, hc : hc + state], (1, 1), highest)
    causal = (meta[:, 0:1] == row_ref[0:1, :]) & (iota((span, span), 0) >= iota((span, span), 1))
    per = LANES // hs
    lane = iota((span, LANES), 1) // hs
    for tile in range(hc // LANES):
        lanes = pl.ds(tile * LANES, LANES)
        x = act_ref[:, lanes]
        scaled = (x * spread(step, tile * per, per, hs)).astype(bf16)
        y = skip_ref[0:1, lanes] * x
        for k in range(per):
            h = tile * per + k
            decay = jnp.where(causal, jnp.exp(running[:, h : h + 1] - running_t[h : h + 1, :]), 0.0)
            mixing = (gram * decay).astype(bf16)
            y = y + dot(mixing, jnp.where(lane == k, scaled, jnp.zeros_like(scaled)), (1, 0))
        y_ref[:, lanes] = y


def gate_kernel(u_ref, wg_ref, cot_ref, wo_ref, y_ref, gate_ref, back_ref, sums_ref):
    gate = jnp.dot(u_ref[...], wg_ref[...], preferred_element_type=f32)
    back = dot(cot_ref[...], wo_ref[...], (1, 1))
    gated = y_ref[...] * (gate * sigmoid(gate))
    ones = jnp.ones((8, gated.shape[1]), f32)
    gate_ref[...] = gate
    back_ref[...] = back
    sums_ref[0:8, :] = dot(ones, gated * gated, (1, 1), highest)
    sums_ref[8:16, :] = dot(ones, gated * back, (1, 1), highest)


def norm_kernel(y_ref, gate_ref, back_ref, sums_ref, mix_ref, dgate_ref, dy_ref, *, width):
    span = y_ref.shape[0]
    eye = (iota((span, span), 0) == iota((span, span), 1)).astype(f32)
    columns = dot(eye, sums_ref[...], (1, 1), highest)
    scale = lax.rsqrt(columns[:, 0:1] / width + norm_eps)
    pull = scale * scale * scale * (columns[:, 8:9] / width)
    y = y_ref[...]
    gate = gate_ref[...]
    sig = sigmoid(gate)
    gated = y * (gate * sig)
    mix_ref[...] = (gated * scale).astype(bf16)
    grad = scale * back_ref[...] - pull * gated
    dy_ref[...] = (grad * (gate * sig)).astype(bf16)
    dgate_ref[...] = (grad * y * (sig * (1.0 + gate * (1.0 - sig)))).astype(bf16)


def backward_kernel(
    p_ref, y_ref, dy_ref, conv_ref, heads_ref, skip_ref, meta_ref, row_ref,
    dp_ref, dconv_ref, dheads_ref, dskip_ref, act_ref, slope_ref, dact_ref, *, dims,
):
    hc, state, hs, taps = dims
    span = p_ref.shape[0]
    wide = hc + 2 * state

    @pl.when(pl.program_id(0) == 0)
    def _():
        dconv_ref[...] = jnp.zeros_like(dconv_ref)
        dheads_ref[...] = jnp.zeros_like(dheads_ref)
        dskip_ref[...] = jnp.zeros_like(dskip_ref)

    meta = meta_ref[...]
    for c in range(0, wide, 2 * LANES):
        lanes = pl.ds(c, min(2 * LANES, wide - c))
        conv = conv_piece(p_ref[:, lanes], meta, conv_ref, lanes, taps)
        sig = sigmoid(conv)
        act_ref[:, lanes] = conv * sig
        slope_ref[:, lanes] = sig * (1.0 + conv * (1.0 - sig))
    pre, step, log_decay, running, running_t = rates(p_ref[:, wide : wide + LANES], heads_ref)
    bmat = act_ref[:, hc : hc + state]
    cmat = act_ref[:, hc + state : wide]
    gram_t = dot(bmat, cmat, (1, 1), highest)
    causal_t = (meta[:, 0:1] == row_ref[0:1, :]) & (iota((span, span), 0) <= iota((span, span), 1))
    per = LANES // hs
    lane = iota((span, LANES), 1) // hs
    dgram_t = jnp.zeros((span, span), f32)
    drun = jnp.zeros((span, LANES), f32)
    dstep = jnp.zeros((span, LANES), f32)
    for tile in range(hc // LANES):
        lanes = pl.ds(tile * LANES, LANES)
        x = act_ref[:, lanes]
        spread_step = spread(step, tile * per, per, hs)
        scaled = (x * spread_step).astype(bf16)
        dy = dy_ref[:, lanes]
        dscaled = jnp.zeros((span, LANES), f32)
        for k in range(per):
            h = tile * per + k
            decay_t = jnp.where(causal_t, jnp.exp(running_t[h : h + 1, :] - running[:, h : h + 1]), 0.0)
            mixing_t = (gram_t * decay_t).astype(bf16)
            own = lane == k
            dmix_t = dot(jnp.where(own, scaled, jnp.zeros_like(scaled)), dy, (1, 1))
            dgram_t = dgram_t + dmix_t * decay_t
            dscaled = dscaled + dot(mixing_t, jnp.where(own, dy, jnp.zeros_like(dy)), (1, 0))
        dy = dy.astype(f32)
        skip = skip_ref[0:1, lanes]
        to_head = (iota((LANES, LANES), 0) // hs + tile * per == iota((LANES, LANES), 1)).astype(f32)
        drun = drun + dot(dy * (y_ref[:, lanes] - skip * x) - scaled.astype(f32) * dscaled, to_head, (1, 0), highest)
        dstep = dstep + dot(dscaled * x, to_head, (1, 0), highest)
        dskip_ref[0:1, lanes] += jnp.sum(dy * x, axis=0, keepdims=True)
        dact_ref[:, lanes] = dscaled * spread_step + skip * dy
    half = dgram_t.astype(bf16)
    dact_ref[:, hc : hc + state] = dot(half, cmat.astype(bf16), (1, 0))
    dact_ref[:, hc + state : wide] = dot(half, bmat.astype(bf16), (0, 0))
    upper = (iota((span, span), 0) <= iota((span, span), 1)).astype(f32)
    dlog = dot(upper, drun, (1, 0), highest)
    draw = (dstep + dlog * heads_ref[0:1, :]) * sigmoid(pre)
    dheads_ref[0:1, :] += jnp.sum(dlog * log_decay, axis=0, keepdims=True)
    dheads_ref[1:2, :] += jnp.sum(draw, axis=0, keepdims=True)
    dp_ref[:, wide : wide + LANES] = draw.astype(bf16)
    for c in range(0, wide, 2 * LANES):
        lanes = pl.ds(c, min(2 * LANES, wide - c))
        raw = p_ref[:, lanes]
        grad = dact_ref[:, lanes] * slope_ref[:, lanes]
        back = conv_ref[0:1, lanes] * grad
        dconv_ref[0:1, lanes] += jnp.sum(grad * raw, axis=0, keepdims=True)
        dconv_ref[taps : taps + 1, lanes] += jnp.sum(grad, axis=0, keepdims=True)
        for k in range(1, taps):
            masked = meta[:, k : k + 1] * grad
            back = back + conv_ref[k : k + 1, lanes] * pltpu.roll(masked, span - k, 0)
            dconv_ref[k : k + 1, lanes] += jnp.sum(masked * pltpu.roll(raw, k, 0), axis=0, keepdims=True)
        dp_ref[:, lanes] = back.astype(bf16)


def adam_update(weight, first, second, gradient, rate):
    first_new = beta_first * first + (1.0 - beta_first) * gradient
    second_new = beta_second * second + (1.0 - beta_second) * gradient * gradient
    first_hat = first_new / (1.0 - beta_first**STEP)
    second_hat = second_new / (1.0 - beta_second**STEP)
    weight_new = weight - rate * (first_hat / (jnp.sqrt(second_hat) + adam_eps) + weight_decay * weight)
    return (weight_new, first_new, second_new)


def adam_in_kernel(
    me_ref, a_ref, b_ref, tail_ref, gain_ref, w_ref, f_ref, s_ref, g_out, w_out, f_out, s_out, gain_out, *, tiles, width
):
    i = pl.program_id(0)
    raw = jnp.where(
        i < tiles, a_ref[0].astype(f32), jnp.where(i < 2 * tiles, b_ref[0].astype(f32), tail_ref[...])
    )
    gain = gain_ref[...]
    w = w_ref[...]
    grad = gain * raw
    g_out[...] = grad
    w_out[...], f_out[...], s_out[...] = adam_update(w, f_ref[...], s_ref[...], grad, matrix_rate)

    @pl.when(i == 0)
    def _():
        gain_out[...] = jnp.zeros_like(gain_out)

    inside = iota(raw.shape, 1) + i * raw.shape[1] < width
    product = jnp.where(inside, w.astype(bf16).astype(f32) * raw, 0.0)
    gain_out[...] += jnp.sum(product, axis=1, keepdims=True)


def adam_out_kernel(me_ref, a_ref, gain_ref, w_ref, f_ref, s_ref, g_out, w_out, f_out, s_out, gain_out):
    raw = a_ref[0].astype(f32)
    w = w_ref[...]
    grad = gain_ref[...] * raw
    g_out[...] = grad
    w_out[...], f_out[...], s_out[...] = adam_update(w, f_ref[...], s_ref[...], grad, matrix_rate)
    gain_out[...] = jnp.sum(w.astype(bf16).astype(f32) * raw, axis=1, keepdims=True)


def cost(flops, nbytes, transcendentals=0):
    return pl.CostEstimate(flops=flops, bytes_accessed=nbytes, transcendentals=transcendentals)


def shape(dims, dtype=f32):
    return jax.ShapeDtypeStruct(dims, dtype)


def rows_spec(span, width):
    return pl.BlockSpec((span, width), lambda g: (g, 0))


def whole_spec(dims):
    return pl.BlockSpec(dims, lambda g: (0,) * len(dims))


def run(
    reps, shards,
    tokens, cotangent, segment, live_rows,
    in_weight, out_weight, conv_table, norm_in, norm_gate, head_params,
    in_first, out_first, conv_first, norm_in_first, norm_gate_first, heads_first,
    in_second, out_second, conv_second, norm_in_second, norm_gate_second, heads_second,
):
    own_rows, width = tokens.shape
    span = own_rows // live_rows.shape[0]
    rows = own_rows * reps
    groups = rows // span
    inner = norm_gate.shape[0] * shards
    taps = conv_table.shape[0] - 1
    piece = conv_table.shape[1]
    channels = piece * shards
    heads = head_params.shape[1]
    hs = inner // heads
    state = (channels - inner) // 2
    hr = heads // reps
    hc = inner // reps
    wide = hc + 2 * state
    dl = in_weight.shape[0]
    projections = in_weight.shape[1]
    rep = lax.axis_index("rep")
    me = lax.axis_index("shard")
    dims = (hc, state, hs, taps)

    gain_in = norm_in.astype(bf16).astype(f32)[:, None]
    gain_gate = norm_gate.astype(bf16).astype(f32)[:, None]

    def copy(values, gain):
        return (values.astype(bf16).astype(f32) * gain).astype(bf16)

    x_columns = lax.dynamic_slice(in_weight, (0, inner + hc * rep), (dl, hc))
    step_columns = lax.dynamic_slice(in_weight[:, inner + channels :], (0, hr * rep), (dl, hr))
    wx_own = copy(
        jnp.concatenate(
            [
                x_columns,
                in_weight[:, 2 * inner : 2 * inner + 2 * state],
                jnp.pad(step_columns, ((0, 0), (0, LANES - hr))),
            ],
            axis=1,
        ),
        gain_in,
    )
    wg_own = copy(lax.dynamic_slice(in_weight, (0, hc * rep), (dl, hc)), gain_in)
    out_rows = out_weight.shape[0] // reps
    wo_piece = copy(
        lax.dynamic_slice(out_weight, (out_rows * rep, 0), (out_rows, width)),
        lax.dynamic_slice(gain_gate, (out_rows * rep, 0), (out_rows, 1)),
    )
    deal = [(r * shards + s, s * reps + r) for r in range(reps) for s in range(shards)]
    collect = [(b, a) for a, b in deal]

    live = (jnp.arange(own_rows) % span < jnp.repeat(live_rows, span))[:, None]
    values = jnp.where(live, tokens.astype(f32), 0.0)
    scale_in = lax.rsqrt(jnp.mean(values * values, axis=1, keepdims=True) + norm_eps)
    u_own = (values * scale_in).astype(bf16)
    cot_own = jnp.where(live, cotangent, jnp.zeros_like(cotangent))
    segments = jnp.concatenate(rep_gather(segment, reps)).reshape(groups, span)
    u = jnp.concatenate(rep_gather(u_own, reps))
    cot = jnp.concatenate(rep_gather(cot_own, reps))
    place = jnp.arange(span)[None, :]
    meta = [segments.astype(f32)]
    for k in range(1, taps):
        meta.append(((jnp.roll(segments, k, axis=1) == segments) & (place >= k)).astype(f32))
    meta = jnp.pad(jnp.stack(meta, axis=-1).reshape(rows, taps), ((0, 0), (0, 8 - taps)))
    row_meta = jnp.broadcast_to(segments.astype(f32).reshape(1, rows), (8, rows))

    conv_all = jnp.zeros((8, channels), f32)
    conv_all = lax.dynamic_update_slice(
        conv_all, jnp.pad(conv_table.astype(bf16).astype(f32), ((0, 7 - taps), (0, 0))), (0, piece * me)
    )
    conv_all = sum_shards(conv_all, shards)
    conv = jnp.concatenate([lax.dynamic_slice(conv_all, (0, hc * rep), (8, hc)), conv_all[:, inner:]], axis=1)
    own_heads = lax.dynamic_slice(head_params, (0, hr * rep), (3, hr))
    head_rows = jnp.pad(jnp.stack([-jnp.exp(own_heads[0]), own_heads[2]]), ((0, 6), (0, LANES - hr)))
    skip = jnp.broadcast_to(jnp.repeat(own_heads[1], hs)[None], (8, hc))

    wx = gather_shards(wx_own, shards)
    wg = gather_shards(wg_own, shards)
    wo = gather_shards(lax.ppermute(wo_piece, ("rep", "shard"), deal), shards)

    p, y = pl.pallas_call(
        functools.partial(forward_kernel, dims=dims),
        grid=(groups,),
        in_specs=[
            rows_spec(span, width), whole_spec(wx.shape), whole_spec(conv.shape), whole_spec(head_rows.shape),
            whole_spec(skip.shape), rows_spec(span, 8), pl.BlockSpec((8, span), lambda g: (0, g)),
        ],
        out_specs=[rows_spec(span, wide + LANES), rows_spec(span, hc)],
        out_shape=[shape((rows, wide + LANES)), shape((rows, hc))],
        scratch_shapes=[pltpu.VMEM((span, wide), f32)],
        cost_estimate=cost(2 * rows * width * (wide + LANES), 12 << 20, rows * span * hr),
        name="mixer_forward",
    )(u, wx, conv, head_rows, skip, meta, row_meta)

    gate, back, sums = pl.pallas_call(
        gate_kernel,
        grid=(groups,),
        in_specs=[
            rows_spec(span, width), whole_spec(wg.shape), rows_spec(span, width), whole_spec(wo.shape),
            rows_spec(span, hc),
        ],
        out_specs=[rows_spec(span, hc), rows_spec(span, hc), pl.BlockSpec((16, span), lambda g: (0, g))],
        out_shape=[shape((rows, hc)), shape((rows, hc)), shape((16, rows))],
        cost_estimate=cost(4 * rows * width * hc, 20 << 20, rows * hc),
        name="gate_forward",
    )(u, wg, cot, wo, y)
    for bit in rep_bits(reps):
        there = rep_swap(sums, bit, reps)
        order = [there[:, (j ^ bit) * own_rows : ((j ^ bit) + 1) * own_rows] for j in range(reps)]
        sums = sums + jnp.concatenate(order, axis=1)

    mix, dgate, dy = pl.pallas_call(
        functools.partial(norm_kernel, width=inner),
        grid=(groups,),
        in_specs=[rows_spec(span, hc)] * 3 + [pl.BlockSpec((16, span), lambda g: (0, g))],
        out_specs=[rows_spec(span, hc)] * 3,
        out_shape=[shape((rows, hc), bf16)] * 3,
        cost_estimate=cost(20 * rows * hc, 15 << 20, rows * hc),
        name="gate_backward",
    )(y, gate, back, sums)

    branch = dot(mix, wo, (1, 0)).astype(bf16).reshape(reps, own_rows, width)
    grad_out_part = dot(mix, cot, (0, 0)).astype(bf16).reshape(shards, hc // shards, width)
    grad_gate_part = dot(u, dgate, (0, 0)).astype(bf16).reshape(shards, dl, hc)
    out_sum = reduce_shards(grad_out_part, shards).astype(bf16)
    out_sum = lax.ppermute(out_sum, ("rep", "shard"), collect)
    out_sums = jnp.stack(rep_gather(out_sum, reps))
    gate_sums = jnp.stack(rep_gather(reduce_shards(grad_gate_part, shards).astype(bf16), reps))
    branch_sum = rep_scatter_sum([branch[j] for j in range(reps)], reps, bf16)
    block_out = (values + branch_sum).astype(bf16)

    dp, dconv, dheads, dskip = pl.pallas_call(
        functools.partial(backward_kernel, dims=dims),
        grid=(groups,),
        in_specs=[
            rows_spec(span, wide + LANES), rows_spec(span, hc), rows_spec(span, hc), whole_spec(conv.shape),
            whole_spec(head_rows.shape), whole_spec(skip.shape), rows_spec(span, 8),
            pl.BlockSpec((8, span), lambda g: (0, g)),
        ],
        out_specs=[
            rows_spec(span, wide + LANES), whole_spec(conv.shape), whole_spec(head_rows.shape),
            whole_spec(skip.shape),
        ],
        out_shape=[shape((rows, wide + LANES), bf16), shape(conv.shape), shape(head_rows.shape), shape(skip.shape)],
        scratch_shapes=[pltpu.VMEM((span, wide), f32)] * 3,
        cost_estimate=cost(4 * rows * span * hc * 2, 12 << 20, rows * span * hr),
        name="mixer_backward",
    )(p, y, dy, conv, head_rows, skip, meta, row_meta)

    head_part = jnp.stack([dheads[0, :hr], jnp.sum(dskip[0].reshape(hr, hs), axis=1), dheads[1, :hr]])
    small = jnp.concatenate([dconv, jnp.pad(head_part, ((0, 5), (0, wide - hr)))], axis=0)
    small = jnp.stack(rep_gather(sum_shards(small, shards), reps))

    grad_x_part = dot(u, dp, (0, 0)).astype(bf16).reshape(shards, dl, wide + LANES)
    x_sums = jnp.stack(rep_gather(reduce_shards(grad_x_part, shards).astype(bf16), reps))
    du = (dot(dgate, wg, (1, 1)) + dot(dp, wx, (1, 1))).astype(bf16).reshape(reps, own_rows, width)
    du = rep_scatter_sum([du[j] for j in range(reps)], reps, bf16)
    scaled = values * scale_in
    pulled = scale_in * (du - scaled * jnp.mean(du * scaled, axis=1, keepdims=True))
    input_grad = jnp.where(live, (cot_own.astype(f32) + pulled).astype(bf16), jnp.zeros_like(cot_own))

    def of_rep(stack, t):
        return lax.dynamic_index_in_dim(stack, t ^ rep, 0, keepdims=False)

    index = rep.astype(jnp.int32)[None]
    tail = jnp.concatenate(
        [jnp.sum(x_sums[:, :, hc:wide].astype(f32), axis=0)]
        + [of_rep(x_sums, t)[:, wide : wide + hr].astype(f32) for t in range(reps)],
        axis=1,
    )
    tile = 3 * LANES
    tiles = inner // tile
    sub = hc // tile
    tail = jnp.pad(tail, ((0, 0), (0, tile - tail.shape[1])))

    def picked(start):
        def index_map(i, me_ref):
            k = jnp.clip(i - start, 0, tiles - 1)
            return ((k // sub) ^ me_ref[0], 0, k % sub)

        return pl.BlockSpec((1, dl, tile), index_map)

    state_spec = pl.BlockSpec((dl, tile), lambda i, me_ref: (0, i))
    column_spec = pl.BlockSpec((dl, 1), lambda i, me_ref: (0, 0))
    grad_in_weight, new_in, new_in_first, new_in_second, in_gain_grad = pl.pallas_call(
        functools.partial(adam_in_kernel, tiles=tiles, width=projections),
        grid_spec=pltpu.PrefetchScalarGridSpec(
            num_scalar_prefetch=1,
            grid=(pl.cdiv(projections, tile),),
            in_specs=[picked(0), picked(tiles), pl.BlockSpec((dl, tile), lambda i, me_ref: (0, 0)), column_spec]
            + [state_spec] * 3,
            out_specs=[state_spec] * 4 + [column_spec],
        ),
        out_shape=[shape(in_weight.shape)] * 4 + [shape((dl, 1))],
        cost_estimate=cost(20 * dl * projections, 30 * dl * projections),
        name="adam_in",
    )(index, gate_sums, x_sums, tail, gain_in, in_weight, in_first, in_second)

    out_spec = pl.BlockSpec((out_rows, width), lambda i, me_ref: (i, 0))
    out_column = pl.BlockSpec((out_rows, 1), lambda i, me_ref: (i, 0))
    grad_out_weight, new_out, new_out_first, new_out_second, out_gain_grad = pl.pallas_call(
        adam_out_kernel,
        grid_spec=pltpu.PrefetchScalarGridSpec(
            num_scalar_prefetch=1,
            grid=(reps,),
            in_specs=[pl.BlockSpec((1, out_rows, width), lambda i, me_ref: (i ^ me_ref[0], 0, 0)), out_column]
            + [out_spec] * 3,
            out_specs=[out_spec] * 4 + [out_column],
        ),
        out_shape=[shape(out_weight.shape)] * 4 + [shape((out_weight.shape[0], 1))],
        cost_estimate=cost(20 * out_weight.size, 30 * out_weight.size),
        name="adam_out",
    )(index, out_sums, gain_gate, out_weight, out_first, out_second)

    ours = [of_rep(small, t) for t in range(reps)]
    conv_grad = jnp.concatenate(
        [v[: taps + 1, :hc] for v in ours] + [jnp.sum(small[:, : taps + 1, hc:], axis=0)], axis=1
    )
    grad_conv = lax.dynamic_slice(conv_grad, (0, piece * me), (taps + 1, piece))
    grad_heads = jnp.concatenate([v[8:11, :hr] for v in ours], axis=1)
    grad_norm_in = in_gain_grad[:, 0]
    grad_norm_gate = out_gain_grad[:, 0]
    new_conv = adam_update(conv_table, conv_first, conv_second, grad_conv, vector_rate)
    new_gin = adam_update(norm_in, norm_in_first, norm_in_second, grad_norm_in, vector_rate)
    new_ggate = adam_update(norm_gate, norm_gate_first, norm_gate_second, grad_norm_gate, vector_rate)
    new_heads = adam_update(head_params, heads_first, heads_second, grad_heads, vector_rate)
    return (
        block_out, input_grad,
        grad_in_weight, grad_out_weight, grad_conv, grad_norm_in, grad_norm_gate, grad_heads,
        new_in, new_out, new_conv[0], new_gin[0], new_ggate[0], new_heads[0],
        new_in_first, new_out_first, new_conv[1], new_gin[1], new_ggate[1], new_heads[1],
        new_in_second, new_out_second, new_conv[2], new_gin[2], new_ggate[2], new_heads[2],
    )


def solution(mesh):
    rows = P(("rep", "shard"), None)
    both = P(("rep", "shard"))
    weights = (P("shard", None), P("shard", None), P(None, "shard"), P("shard"), P("shard"), P())
    return jax.shard_map(
        functools.partial(run, mesh.shape["rep"], mesh.shape["shard"]),
        mesh=mesh,
        in_specs=(rows, rows, both, both) + weights * 3,
        out_specs=(rows, rows) + weights * 4,
        check_vma=False,
    )
```

```python
import functools

import jax
import jax.numpy as jnp
from jax import lax
from jax.experimental import pallas as pl
from jax.experimental.pallas import tpu as pltpu
from jax.sharding import PartitionSpec as P


STEP = 3
norm_eps = 1e-05
beta_first = 0.9
beta_second = 0.95
adam_eps = 1e-08
weight_decay = 0.1
matrix_rate = 0.005
vector_rate = 0.05
highest = lax.Precision.HIGHEST
f32 = jnp.float32
bf16 = jnp.bfloat16
LANES = 128


def dot(a, b, contract, precision=None):
    return lax.dot_general(
        a, b, (((contract[0],), (contract[1],)), ((), ())),
        preferred_element_type=f32, precision=precision,
    )


def rep_swap(x, bit, reps):
    return lax.ppermute(x, "rep", [(i, i ^ bit) for i in range(reps)])


def rep_bits(reps):
    return [1 << k for k in reversed(range(reps.bit_length() - 1))]


def rep_gather(x, reps):
    have = {0: x}
    for bit in rep_bits(reps):
        have.update({j | bit: rep_swap(v, bit, reps) for j, v in list(have.items())})
    return [have[j] for j in range(reps)]


def rep_scatter_sum(blocks, reps, wire):
    have = {j: b for j, b in enumerate(blocks)}
    for bit in reversed(rep_bits(reps)):
        keep = [j for j in have if not j & bit]
        have = {j: have[j].astype(f32) + rep_swap(have[j | bit].astype(wire), bit, reps).astype(f32) for j in keep}
    return have[0]


DEPTH = 4


def lined(shards):
    return shards == 2 * DEPTH


def over_z(moves):
    return [(2 * a + y, 2 * b + y) for a, b in moves for y in range(2)]


UP = over_z([(0, 1), (1, 2), (2, 3)])
DOWN = over_z([(3, 2), (2, 1), (1, 0)])
OUTWARD = over_z([(2, 3), (1, 0)])
RING = {j: over_z([(z, (z + j) % 4) for z in range(4)]) for j in (1, 2, 3)}


def across(zs):
    return [(2 * z + y, 2 * z + 1 - y) for z in zs for y in range(2)]


def gather_shards(block, shards):
    if not lined(shards):
        every = lax.all_gather(block, "shard", axis=0, tiled=False)
        return [(i, every[i]) for i in range(shards)]
    me = lax.axis_index("shard")
    z, y = me // 2, me % 2
    far_own = lax.ppermute(block, "shard", across(range(4)))
    up = lax.ppermute(block, "shard", UP)
    down = lax.ppermute(block, "shard", DOWN)
    two = lax.ppermute(block, "shard", RING[2])
    third = lax.ppermute(two, "shard", OUTWARD)
    far_up = lax.ppermute(up, "shard", across((1, 2, 3)))
    far_down = lax.ppermute(down, "shard", across((0, 1, 2)))
    far_two = lax.ppermute(two, "shard", across(range(4)))
    far_third = lax.ppermute(third, "shard", across((0, 3)))
    at_third = jnp.where(z == 0, 3, jnp.where(z == 3, 0, z))
    found = []
    for where, value, far in (
        ((z + 3) % 4, up, far_up),
        ((z + 1) % 4, down, far_down),
        ((z + 2) % 4, two, far_two),
        (at_third, third, far_third),
        (z, block, far_own),
    ):
        found += [(2 * where + y, value), (2 * where + 1 - y, far)]
    return found


def placed(found, shards, pick):
    first = pick(found[0][1])
    full = jnp.zeros((shards, *first.shape), first.dtype)
    for index, value in found:
        full = lax.dynamic_update_slice(full, pick(value)[None], (index, 0, 0))
    return full


def reduce_shards(parts, shards):
    if not lined(shards):
        return lax.psum_scatter(parts, "shard", scatter_dimension=0, tiled=True)[0].astype(f32)
    me = lax.axis_index("shard")
    z, y = me // 2, me % 2

    def block(j, side):
        return lax.dynamic_index_in_dim(parts, 2 * ((z + j) % 4) + side, 0, keepdims=False)

    def far(js):
        value = jnp.stack([block(j, 1 - y) for j in js])
        return lax.ppermute(value, "shard", across(range(4))).astype(f32)

    def ring(j, got):
        value = (block(j, y).astype(f32) + got).astype(bf16)
        return lax.ppermute(value, "shard", RING[j]).astype(f32)

    middle, sides, here = far((2,)), far((1, 3)), far((0,))
    total = block(0, y).astype(f32) + here[0]
    return total + ring(2, middle[0]) + ring(1, sides[0]) + ring(3, sides[1])


def sum_shards(x, shards):
    if shards & (shards - 1):
        return lax.psum(x, "shard")
    for bit in (1 << k for k in range(shards.bit_length() - 1)):
        x = x + lax.ppermute(x, "shard", [(i, i ^ bit) for i in range(shards)])
    return x


def softplus(v):
    return jnp.maximum(v, 0.0) + jnp.log1p(jnp.exp(-jnp.abs(v)))


def sigmoid(v):
    return 1.0 / (1.0 + jnp.exp(-v))


def iota(shape, axis):
    return lax.broadcasted_iota(jnp.int32, shape, axis)


PIECE = 2 * LANES


def sequences(row_ref, taps):
    span = row_ref.shape[1]
    number = jnp.broadcast_to(row_ref[0:1, :], (LANES, span)).T
    number = jnp.concatenate([number] * (PIECE // LANES), axis=1)
    row = iota(number.shape, 0)
    same = [((pltpu.roll(number, k, 0) == number) & (row >= k)).astype(f32) for k in range(1, taps)]
    return number, [None] + same


def conv_piece(raw, same, conv_ref, lanes, taps):
    total = conv_ref[taps : taps + 1, lanes] + conv_ref[0:1, lanes] * raw
    for k in range(1, taps):
        total = total + conv_ref[k : k + 1, lanes] * (same[k] * pltpu.roll(raw, k, 0))
    return total


def rates(raw, heads_ref):
    span = raw.shape[0]
    pre = raw + heads_ref[1:2, :]
    step = softplus(pre)
    log_decay = step * heads_ref[0:1, :]
    lower = (iota((span, span), 0) >= iota((span, span), 1)).astype(f32)
    running = dot(lower, log_decay, (1, 0), highest)
    return pre, step, log_decay, running, running.T


def spread(columns, first, count, head_size):
    lane = iota((columns.shape[0], LANES), 1) // head_size
    value = jnp.broadcast_to(columns[:, first : first + 1], lane.shape)
    for k in range(1, count):
        value = jnp.where(lane == k, columns[:, first + k : first + k + 1], value)
    return value


def forward_kernel(u_ref, w_ref, conv_ref, heads_ref, skip_ref, row_ref, p_ref, y_ref, act_ref, *, dims):
    hc, state, hs, taps = dims
    span = u_ref.shape[0]
    wide = hc + 2 * state
    p_ref[...] = jnp.dot(u_ref[...], w_ref[...], preferred_element_type=f32)
    number, same = sequences(row_ref, taps)
    for c in range(0, wide, PIECE):
        lanes = pl.ds(c, PIECE)
        conv = conv_piece(p_ref[:, lanes], same, conv_ref, lanes, taps)
        act_ref[:, lanes] = conv * sigmoid(conv)
    _, step, _, running, running_t = rates(p_ref[:, wide : wide + LANES], heads_ref)
    gram = dot(act_ref[:, hc + state : wide], act_ref[:, hc : hc + state], (1, 1), highest)
    causal = (number[:, 0:1] == row_ref[0:1, :]) & (iota((span, span), 0) >= iota((span, span), 1))
    per = LANES // hs
    lane = iota((span, LANES), 1) // hs
    for tile in range(hc // LANES):
        lanes = pl.ds(tile * LANES, LANES)
        x = act_ref[:, lanes]
        scaled = (x * spread(step, tile * per, per, hs)).astype(bf16)
        y = skip_ref[0:1, lanes] * x
        for k in range(per):
            h = tile * per + k
            decay = jnp.where(causal, jnp.exp(running[:, h : h + 1] - running_t[h : h + 1, :]), 0.0)
            mixing = (gram * decay).astype(bf16)
            y = y + dot(mixing, jnp.where(lane == k, scaled, jnp.zeros_like(scaled)), (1, 0))
        y_ref[:, lanes] = y


def gate_kernel(u_ref, wg_ref, cot_ref, wo_ref, y_ref, gate_ref, back_ref, sums_ref):
    gate = jnp.dot(u_ref[...], wg_ref[...], preferred_element_type=f32)
    back = dot(cot_ref[...], wo_ref[...], (1, 1))
    gated = y_ref[...] * (gate * sigmoid(gate))
    ones = jnp.ones((8, gated.shape[1]), f32)
    gate_ref[...] = gate
    back_ref[...] = back
    sums_ref[0:8, :] = dot(ones, gated * gated, (1, 1), highest)
    sums_ref[8:16, :] = dot(ones, gated * back, (1, 1), highest)


def norm_kernel(y_ref, gate_ref, back_ref, sums_ref, mix_ref, dgate_ref, dy_ref, *, width):
    span = y_ref.shape[0]
    eye = (iota((span, span), 0) == iota((span, span), 1)).astype(f32)
    columns = dot(eye, sums_ref[...], (1, 1), highest)
    scale = lax.rsqrt(columns[:, 0:1] / width + norm_eps)
    pull = scale * scale * scale * (columns[:, 8:9] / width)
    y = y_ref[...]
    gate = gate_ref[...]
    sig = sigmoid(gate)
    gated = y * (gate * sig)
    mix_ref[...] = (gated * scale).astype(bf16)
    grad = scale * back_ref[...] - pull * gated
    dy_ref[...] = (grad * (gate * sig)).astype(bf16)
    dgate_ref[...] = (grad * y * (sig * (1.0 + gate * (1.0 - sig)))).astype(bf16)


def backward_kernel(
    p_ref, y_ref, dy_ref, conv_ref, heads_ref, skip_ref, row_ref,
    dp_ref, dconv_ref, dheads_ref, dskip_ref, act_ref, slope_ref, dact_ref, *, dims,
):
    hc, state, hs, taps = dims
    span = p_ref.shape[0]
    wide = hc + 2 * state

    @pl.when(pl.program_id(0) == 0)
    def _():
        dconv_ref[...] = jnp.zeros_like(dconv_ref)
        dheads_ref[...] = jnp.zeros_like(dheads_ref)
        dskip_ref[...] = jnp.zeros_like(dskip_ref)

    number, same = sequences(row_ref, taps)
    for c in range(0, wide, PIECE):
        lanes = pl.ds(c, PIECE)
        conv = conv_piece(p_ref[:, lanes], same, conv_ref, lanes, taps)
        sig = sigmoid(conv)
        act_ref[:, lanes] = conv * sig
        slope_ref[:, lanes] = sig * (1.0 + conv * (1.0 - sig))
    pre, step, log_decay, running, running_t = rates(p_ref[:, wide : wide + LANES], heads_ref)
    bmat = act_ref[:, hc : hc + state]
    cmat = act_ref[:, hc + state : wide]
    gram_t = dot(bmat, cmat, (1, 1), highest)
    causal_t = (number[:, 0:1] == row_ref[0:1, :]) & (iota((span, span), 0) <= iota((span, span), 1))
    per = LANES // hs
    lane = iota((span, LANES), 1) // hs
    dgram_t = jnp.zeros((span, span), f32)
    drun = jnp.zeros((span, LANES), f32)
    dstep = jnp.zeros((span, LANES), f32)
    for tile in range(hc // LANES):
        lanes = pl.ds(tile * LANES, LANES)
        x = act_ref[:, lanes]
        spread_step = spread(step, tile * per, per, hs)
        scaled = (x * spread_step).astype(bf16)
        dy = dy_ref[:, lanes]
        dscaled = jnp.zeros((span, LANES), f32)
        for k in range(per):
            h = tile * per + k
            decay_t = jnp.where(causal_t, jnp.exp(running_t[h : h + 1, :] - running[:, h : h + 1]), 0.0)
            mixing_t = (gram_t * decay_t).astype(bf16)
            own = lane == k
            dmix_t = dot(jnp.where(own, scaled, jnp.zeros_like(scaled)), dy, (1, 1))
            dgram_t = dgram_t + dmix_t * decay_t
            dscaled = dscaled + dot(mixing_t, jnp.where(own, dy, jnp.zeros_like(dy)), (1, 0))
        dy = dy.astype(f32)
        skip = skip_ref[0:1, lanes]
        to_head = (iota((LANES, LANES), 0) // hs + tile * per == iota((LANES, LANES), 1)).astype(f32)
        drun = drun + dot(dy * (y_ref[:, lanes] - skip * x) - scaled.astype(f32) * dscaled, to_head, (1, 0), highest)
        dstep = dstep + dot(dscaled * x, to_head, (1, 0), highest)
        dskip_ref[0:1, lanes] += jnp.sum(dy * x, axis=0, keepdims=True)
        dact_ref[:, lanes] = dscaled * spread_step + skip * dy
    half = dgram_t.astype(bf16)
    dact_ref[:, hc : hc + state] = dot(half, cmat.astype(bf16), (1, 0))
    dact_ref[:, hc + state : wide] = dot(half, bmat.astype(bf16), (0, 0))
    upper = (iota((span, span), 0) <= iota((span, span), 1)).astype(f32)
    dlog = dot(upper, drun, (1, 0), highest)
    draw = (dstep + dlog * heads_ref[0:1, :]) * sigmoid(pre)
    dheads_ref[0:1, :] += jnp.sum(dlog * log_decay, axis=0, keepdims=True)
    dheads_ref[1:2, :] += jnp.sum(draw, axis=0, keepdims=True)
    dp_ref[:, wide : wide + LANES] = draw.astype(bf16)
    for c in range(0, wide, PIECE):
        lanes = pl.ds(c, PIECE)
        raw = p_ref[:, lanes]
        grad = dact_ref[:, lanes] * slope_ref[:, lanes]
        back = conv_ref[0:1, lanes] * grad
        dconv_ref[0:1, lanes] += jnp.sum(grad * raw, axis=0, keepdims=True)
        dconv_ref[taps : taps + 1, lanes] += jnp.sum(grad, axis=0, keepdims=True)
        for k in range(1, taps):
            masked = same[k] * grad
            back = back + conv_ref[k : k + 1, lanes] * pltpu.roll(masked, span - k, 0)
            dconv_ref[k : k + 1, lanes] += jnp.sum(masked * pltpu.roll(raw, k, 0), axis=0, keepdims=True)
        dp_ref[:, lanes] = back.astype(bf16)


def grad_b_kernel(u_ref, dgate_ref, mix_ref, cot_ref, out_ref):
    count, rows, hc = out_ref.shape
    gate = dot(u_ref[...], dgate_ref[...], (0, 0)).astype(bf16)
    dl = gate.shape[0] // count
    out_ref[:, :dl, :] = gate.reshape(count, dl, hc)
    outer = dot(mix_ref[...], cot_ref[...], (0, 0)).astype(bf16)
    piece = outer.shape[0] // count
    for k in range((rows - dl) // piece):
        out_ref[:, dl + k * piece : dl + (k + 1) * piece, :] = outer[:, k * hc : (k + 1) * hc].reshape(count, piece, hc)


def turn_kernel(w_ref, out_ref):
    out_ref[...] = w_ref[...].astype(f32).T


def branch_kernel(mix_ref, wo_ref, out_ref):
    out_ref[...] = jnp.dot(mix_ref[...], wo_ref[...], preferred_element_type=f32).astype(bf16)


def du_kernel(dgate_ref, wg_ref, dp_ref, wx_ref, out_ref):
    out_ref[...] = (dot(dgate_ref[...], wg_ref[...], (1, 1)) + dot(dp_ref[...], wx_ref[...], (1, 1))).astype(bf16)


def adam_update(weight, first, second, gradient, rate):
    first_new = beta_first * first + (1.0 - beta_first) * gradient
    second_new = beta_second * second + (1.0 - beta_second) * gradient * gradient
    first_hat = first_new * (1.0 / (1.0 - beta_first**STEP))
    second_hat = second_new * (1.0 / (1.0 - beta_second**STEP))
    weight_new = weight - rate * (first_hat / (jnp.sqrt(second_hat) + adam_eps) + weight_decay * weight)
    return (weight_new, first_new, second_new)


def adam_gate_kernel(me_ref, a_ref, gain_ref, w_ref, f_ref, s_ref, g_out, w_out, f_out, s_out, gain_out):
    @pl.when(pl.program_id(0) == 0)
    def _():
        gain_out[...] = jnp.zeros_like(gain_out)

    raw = a_ref[0].astype(f32)
    w = w_ref[...]
    grad = gain_ref[...] * raw
    g_out[...] = grad
    w_out[...], f_out[...], s_out[...] = adam_update(w, f_ref[...], s_ref[...], grad, matrix_rate)
    gain_out[...] += jnp.sum(w.astype(bf16).astype(f32) * raw, axis=1, keepdims=True)


def adam_rest_kernel(
    me_ref, a_ref, tail_ref, part_ref, gain_ref, w_ref, f_ref, s_ref, g_in, w_in, f_in, s_in,
    g_out, w_out, f_out, s_out, gain_out, *, start, tiles, width,
):
    i = pl.program_id(0)

    @pl.when(i == 0)
    def _():
        gain_out[...] = part_ref[...]

    raw = jnp.where(i < tiles, a_ref[0].astype(f32), tail_ref[...])
    w = w_ref[...]
    grad = gain_ref[...] * raw
    g_out[...] = grad
    w_out[...], f_out[...], s_out[...] = adam_update(w, f_ref[...], s_ref[...], grad, matrix_rate)
    inside = iota(raw.shape, 1) + (i + start) * raw.shape[1] < width
    product = jnp.where(inside, w.astype(bf16).astype(f32) * raw, 0.0)
    gain_out[...] += jnp.sum(product, axis=1, keepdims=True)


def adam_out_kernel(me_ref, a_ref, gain_ref, w_ref, f_ref, s_ref, g_out, w_out, f_out, s_out, gain_out):
    rows, columns = w_ref.shape
    chunks = columns // a_ref.shape[2]
    first = a_ref.shape[1] - rows * chunks
    raw = jnp.concatenate(
        [a_ref[0, first + k * rows : first + (k + 1) * rows, :] for k in range(chunks)], axis=1
    ).astype(f32)
    w = w_ref[...]
    grad = gain_ref[...] * raw
    g_out[...] = grad
    w_out[...], f_out[...], s_out[...] = adam_update(w, f_ref[...], s_ref[...], grad, matrix_rate)
    gain_out[...] = jnp.sum(w.astype(bf16).astype(f32) * raw, axis=1, keepdims=True)


def cost(flops, nbytes, transcendentals=0):
    return pl.CostEstimate(flops=flops, bytes_accessed=nbytes, transcendentals=transcendentals)


def shape(dims, dtype=f32):
    return jax.ShapeDtypeStruct(dims, dtype)


def kernel(body, **settings):
    return pl.pallas_call(body, **settings)


def rows_spec(span, width):
    return pl.BlockSpec((span, width), lambda g: (g, 0))


def whole_spec(dims):
    return pl.BlockSpec(dims, lambda g: (0,) * len(dims))


def run(
    reps, shards,
    tokens, cotangent, segment, live_rows,
    in_weight, out_weight, conv_table, norm_in, norm_gate, head_params,
    in_first, out_first, conv_first, norm_in_first, norm_gate_first, heads_first,
    in_second, out_second, conv_second, norm_in_second, norm_gate_second, heads_second,
):
    own_rows, width = tokens.shape
    span = own_rows // live_rows.shape[0]
    rows = own_rows * reps
    groups = rows // span
    inner = norm_gate.shape[0] * shards
    taps = conv_table.shape[0] - 1
    piece = conv_table.shape[1]
    channels = piece * shards
    heads = head_params.shape[1]
    hs = inner // heads
    state = (channels - inner) // 2
    hr = heads // reps
    hc = inner // reps
    wide = hc + 2 * state
    dl = in_weight.shape[0]
    projections = in_weight.shape[1]
    rep = lax.axis_index("rep")
    me = lax.axis_index("shard")
    dims = (hc, state, hs, taps)

    gain_in = norm_in.astype(bf16).astype(f32)[:, None]
    gain_gate = norm_gate.astype(bf16).astype(f32)[:, None]

    def copy(values, gain):
        return (values.astype(bf16).astype(f32) * gain).astype(bf16)

    x_columns = lax.dynamic_slice(in_weight, (0, inner + hc * rep), (dl, hc))
    step_columns = lax.dynamic_slice(in_weight[:, inner + channels :], (0, hr * rep), (dl, hr))
    folds = pl.cdiv(piece, dl)
    conv_lane = hr + -hr % 16
    conv_own = jnp.pad(conv_table.astype(bf16), ((0, 0), (0, folds * dl - piece)))
    conv_own = conv_own.reshape(taps + 1, folds, dl).transpose(2, 1, 0).reshape(dl, folds * (taps + 1))
    wx_own = jnp.concatenate(
        [
            copy(x_columns, gain_in),
            copy(in_weight[:, 2 * inner : 2 * inner + 2 * state], gain_in),
            jnp.pad(copy(step_columns, gain_in), ((0, 0), (0, conv_lane - hr))),
            jnp.pad(conv_own, ((0, 0), (0, LANES - conv_lane - folds * (taps + 1)))),
        ],
        axis=1,
    )
    wg_own = copy(lax.dynamic_slice(in_weight, (0, hc * rep), (dl, hc)), gain_in)
    out_rows = out_weight.shape[0] // reps
    wo_piece = copy(
        lax.dynamic_slice(out_weight, (out_rows * rep, 0), (out_rows, width)),
        lax.dynamic_slice(gain_gate, (out_rows * rep, 0), (out_rows, 1)),
    )
    deal = [(r * shards + s, s * reps + r) for r in range(reps) for s in range(shards)]
    collect = [(b, a) for a, b in deal]

    live = (jnp.arange(own_rows) % span < jnp.repeat(live_rows, span))[:, None]
    values = jnp.where(live, tokens.astype(f32), 0.0)
    scale_in = lax.rsqrt(jnp.mean(values * values, axis=1, keepdims=True) + norm_eps)
    u_own = (values * scale_in).astype(bf16)
    cot_own = jnp.where(live, cotangent, jnp.zeros_like(cotangent))
    numbers = jnp.pad(segment.astype(bf16)[None], ((0, 7), (0, width - own_rows)))
    blocks = rep_gather(jnp.concatenate([u_own, numbers], axis=0), reps)
    u = jnp.concatenate([v[:own_rows] for v in blocks])
    row_numbers = jnp.concatenate([v[own_rows:, :own_rows] for v in blocks], axis=1).astype(f32)
    row_numbers = jnp.broadcast_to(row_numbers[0:1], (8, rows))
    cot = jnp.concatenate(rep_gather(cot_own, reps))

    own_heads = lax.dynamic_slice(head_params, (0, hr * rep), (3, hr))
    head_rows = jnp.pad(jnp.stack([-jnp.exp(own_heads[0]), own_heads[2]]), ((0, 6), (0, LANES - hr)))
    skip = jnp.broadcast_to(jnp.repeat(own_heads[1], hs)[None], (8, hc))

    chunks = width // hc
    wo_own = lax.ppermute(wo_piece, ("rep", "shard"), deal)
    wo_own = [wo_own[:, k * hc : (k + 1) * hc] for k in range(chunks)]
    found_a = gather_shards(wx_own, shards)
    found_b = gather_shards(jnp.concatenate([wg_own, *wo_own], axis=0), shards)
    wx = placed(found_a, shards, lambda v: v).reshape(width, wide + LANES)
    conv_all = kernel(
        turn_kernel,
        grid=(1,),
        in_specs=[pl.BlockSpec((width, LANES), lambda g: (0, wide // LANES))],
        out_specs=whole_spec((LANES, width)),
        out_shape=shape((LANES, width)),
    )(wx)[conv_lane : conv_lane + folds * (taps + 1)]
    conv_all = conv_all.reshape(folds, taps + 1, shards, dl).transpose(1, 2, 0, 3)
    conv_all = conv_all.reshape(taps + 1, shards, folds * dl)[:, :, :piece].reshape(taps + 1, channels)
    conv_all = jnp.pad(conv_all, ((0, 7 - taps), (0, 0)))
    conv = jnp.concatenate([lax.dynamic_slice(conv_all, (0, hc * rep), (8, hc)), conv_all[:, inner:]], axis=1)
    wg = placed(found_b, shards, lambda v: v[:dl]).reshape(width, hc)
    per = hc // shards
    wo = placed(
        found_b, shards,
        lambda v: jnp.concatenate([v[dl + k * per : dl + (k + 1) * per] for k in range(chunks)], axis=1),
    ).reshape(hc, width)

    p, y = kernel(
        functools.partial(forward_kernel, dims=dims),
        grid=(groups,),
        in_specs=[
            rows_spec(span, width), whole_spec(wx.shape), whole_spec(conv.shape), whole_spec(head_rows.shape),
            whole_spec(skip.shape), pl.BlockSpec((8, span), lambda g: (0, g)),
        ],
        out_specs=[rows_spec(span, wide + LANES), rows_spec(span, hc)],
        out_shape=[shape((rows, wide + LANES)), shape((rows, hc))],
        scratch_shapes=[pltpu.VMEM((span, wide), f32)],
        cost_estimate=cost(2 * rows * width * (wide + LANES), 12 << 20, rows * span * hr),
    )(u, wx, conv, head_rows, skip, row_numbers)

    gate, back, sums = kernel(
        gate_kernel,
        grid=(groups,),
        in_specs=[
            rows_spec(span, width), whole_spec(wg.shape), rows_spec(span, width), whole_spec(wo.shape),
            rows_spec(span, hc),
        ],
        out_specs=[rows_spec(span, hc), rows_spec(span, hc), pl.BlockSpec((16, span), lambda g: (0, g))],
        out_shape=[shape((rows, hc)), shape((rows, hc)), shape((16, rows))],
        cost_estimate=cost(4 * rows * width * hc, 20 << 20, rows * hc),
    )(u, wg, cot, wo, y)
    for bit in rep_bits(reps):
        there = rep_swap(sums, bit, reps)
        order = [there[:, (j ^ bit) * own_rows : ((j ^ bit) + 1) * own_rows] for j in range(reps)]
        sums = sums + jnp.concatenate(order, axis=1)

    mix, dgate, dy = kernel(
        functools.partial(norm_kernel, width=inner),
        grid=(groups,),
        in_specs=[rows_spec(span, hc)] * 3 + [pl.BlockSpec((16, span), lambda g: (0, g))],
        out_specs=[rows_spec(span, hc)] * 3,
        out_shape=[shape((rows, hc), bf16)] * 3,
        cost_estimate=cost(20 * rows * hc, 15 << 20, rows * hc),
    )(y, gate, back, sums)

    half = shards // 2
    rows_b = dl + per * chunks
    part_b = kernel(
        grad_b_kernel,
        grid=(2,),
        in_specs=[
            pl.BlockSpec((rows, width // 2), lambda i: (0, i)), whole_spec((rows, hc)),
            pl.BlockSpec((rows, hc // 2), lambda i: (0, i)), whole_spec((rows, width)),
        ],
        out_specs=pl.BlockSpec((half, rows_b, hc), lambda i: (i, 0, 0)),
        out_shape=shape((shards, rows_b, hc), bf16),
        cost_estimate=cost(4 * rows * width * hc, 15 << 20),
    )(u, dgate, mix, cot)
    sum_b = reduce_shards(part_b, shards).astype(bf16)
    out_sum = lax.ppermute(
        jnp.concatenate([sum_b[dl + k * per : dl + (k + 1) * per] for k in range(chunks)], axis=1),
        ("rep", "shard"), collect,
    )
    b_sums = rep_gather(
        jnp.concatenate([sum_b[:dl]] + [out_sum[:, k * hc : (k + 1) * hc] for k in range(chunks)], axis=0), reps
    )
    b_sums = jnp.stack(b_sums)
    branch = kernel(
        branch_kernel,
        grid=(groups,),
        in_specs=[rows_spec(span, hc), whole_spec(wo.shape)],
        out_specs=rows_spec(span, width),
        out_shape=shape((rows, width), bf16),
        cost_estimate=cost(2 * rows * width * hc, 8 << 20),
    )(mix, wo).reshape(reps, own_rows, width)
    branch_sum = rep_scatter_sum([branch[j] for j in range(reps)], reps, bf16)
    block_out = (values + branch_sum).astype(bf16)

    dp, dconv, dheads, dskip = kernel(
        functools.partial(backward_kernel, dims=dims),
        grid=(groups,),
        in_specs=[
            rows_spec(span, wide + LANES), rows_spec(span, hc), rows_spec(span, hc), whole_spec(conv.shape),
            whole_spec(head_rows.shape), whole_spec(skip.shape), pl.BlockSpec((8, span), lambda g: (0, g)),
        ],
        out_specs=[
            rows_spec(span, wide + LANES), whole_spec(conv.shape), whole_spec(head_rows.shape),
            whole_spec(skip.shape),
        ],
        out_shape=[shape((rows, wide + LANES), bf16), shape(conv.shape), shape(head_rows.shape), shape(skip.shape)],
        scratch_shapes=[pltpu.VMEM((span, wide), f32)] * 3,
        cost_estimate=cost(4 * rows * span * hc * 2, 12 << 20, rows * span * hr),
    )(p, y, dy, conv, head_rows, skip, row_numbers)

    head_part = jnp.stack([dheads[0, :hr], jnp.sum(dskip[0].reshape(hr, hs), axis=1), dheads[1, :hr]])
    small = jnp.zeros((8, channels + LANES), f32)
    small = lax.dynamic_update_slice(small, dconv[:, :hc], (0, hc * rep))
    small = lax.dynamic_update_slice(small, dconv[:, hc:], (0, inner))
    small = lax.dynamic_update_slice(small, head_part, (0, channels + hr * rep))
    for bit in reversed(rep_bits(reps)):
        small = small + rep_swap(small, bit, reps)
    small = sum_shards(small, shards)

    part_a = dot(u, dp, (0, 0)).astype(bf16)
    part_a = part_a.reshape(shards, dl, wide + LANES)
    x_sums = jnp.stack(rep_gather(reduce_shards(part_a, shards).astype(bf16), reps))
    du = kernel(
        du_kernel,
        grid=(groups,),
        in_specs=[
            rows_spec(span, hc), whole_spec(wg.shape), rows_spec(span, wide + LANES), whole_spec(wx.shape),
        ],
        out_specs=rows_spec(span, width),
        out_shape=shape((rows, width), bf16),
        cost_estimate=cost(2 * rows * width * (hc + wide + LANES), 12 << 20),
    )(dgate, wg, dp, wx).reshape(reps, own_rows, width)
    du = rep_scatter_sum([du[j] for j in range(reps)], reps, bf16)
    scaled = values * scale_in
    pulled = scale_in * (du - scaled * jnp.mean(du * scaled, axis=1, keepdims=True))
    input_grad = jnp.where(live, (cot_own.astype(f32) + pulled).astype(bf16), jnp.zeros_like(cot_own))

    def of_rep(stack, t):
        return lax.dynamic_index_in_dim(stack, t ^ rep, 0, keepdims=False)

    index = rep.astype(jnp.int32)[None]
    tail = jnp.concatenate(
        [jnp.sum(x_sums[:, :, hc:wide].astype(f32), axis=0)]
        + [of_rep(x_sums, t)[:, wide : wide + hr].astype(f32) for t in range(reps)],
        axis=1,
    )
    tile = hc
    tail = jnp.pad(tail, ((0, 0), (0, tile - tail.shape[1])))

    def picked(i, me_ref):
        return (jnp.minimum(i, reps - 1) ^ me_ref[0], 0, 0)

    def columns(start):
        return pl.BlockSpec((dl, tile), lambda i, me_ref: (0, i + start))

    fixed = lambda i, me_ref: (0, 0)
    row_sum = pl.BlockSpec((dl, 1), fixed)
    in_shapes = [shape(in_weight.shape)] * 4 + [shape((dl, 1))]
    gate_done = kernel(
        adam_gate_kernel,
        grid_spec=pltpu.PrefetchScalarGridSpec(
            num_scalar_prefetch=1,
            grid=(reps,),
            in_specs=[pl.BlockSpec((1, dl, tile), picked), row_sum] + [columns(0)] * 3,
            out_specs=[columns(0)] * 4 + [row_sum],
        ),
        out_shape=in_shapes,
        cost_estimate=cost(20 * dl * inner, 30 * dl * inner),
    )(index, b_sums, gain_in, in_weight, in_first, in_second)
    grad_in_weight, new_in, new_in_first, new_in_second, in_gain_grad = kernel(
        functools.partial(adam_rest_kernel, start=reps, tiles=reps, width=projections),
        grid_spec=pltpu.PrefetchScalarGridSpec(
            num_scalar_prefetch=1,
            grid=(pl.cdiv(projections, tile) - reps,),
            in_specs=[pl.BlockSpec((1, dl, tile), picked), pl.BlockSpec((dl, tile), fixed), row_sum, row_sum]
            + [columns(reps)] * 3
            + [pl.BlockSpec(memory_space=pl.ANY)] * 4,
            out_specs=[columns(reps)] * 4 + [row_sum],
        ),
        out_shape=in_shapes,
        input_output_aliases={8 + k: k for k in range(4)},
        cost_estimate=cost(20 * dl * inner, 30 * dl * inner),
    )(index, x_sums, tail, gate_done[4], gain_in, in_weight, in_first, in_second, *gate_done[:4])

    out_spec = pl.BlockSpec((out_rows, width), lambda i, me_ref: (i, 0))
    out_column = pl.BlockSpec((out_rows, 1), lambda i, me_ref: (i, 0))
    grad_out_weight, new_out, new_out_first, new_out_second, out_gain_grad = kernel(
        adam_out_kernel,
        grid_spec=pltpu.PrefetchScalarGridSpec(
            num_scalar_prefetch=1,
            grid=(reps,),
            in_specs=[pl.BlockSpec((1, *b_sums.shape[1:]), lambda i, me_ref: (i ^ me_ref[0], 0, 0)), out_column]
            + [out_spec] * 3,
            out_specs=[out_spec] * 4 + [out_column],
        ),
        out_shape=[shape(out_weight.shape)] * 4 + [shape((out_weight.shape[0], 1))],
        cost_estimate=cost(20 * out_weight.size, 30 * out_weight.size),
    )(index, b_sums, gain_gate, out_weight, out_first, out_second)

    grad_conv = lax.dynamic_slice(small, (0, piece * me), (taps + 1, piece))
    grad_heads = small[:3, channels : channels + heads]
    grad_norm_in = in_gain_grad[:, 0]
    grad_norm_gate = out_gain_grad[:, 0]
    new_conv = adam_update(conv_table, conv_first, conv_second, grad_conv, vector_rate)
    new_gin = adam_update(norm_in, norm_in_first, norm_in_second, grad_norm_in, vector_rate)
    new_ggate = adam_update(norm_gate, norm_gate_first, norm_gate_second, grad_norm_gate, vector_rate)
    new_heads = adam_update(head_params, heads_first, heads_second, grad_heads, vector_rate)
    return (
        block_out, input_grad,
        grad_in_weight, grad_out_weight, grad_conv, grad_norm_in, grad_norm_gate, grad_heads,
        new_in, new_out, new_conv[0], new_gin[0], new_ggate[0], new_heads[0],
        new_in_first, new_out_first, new_conv[1], new_gin[1], new_ggate[1], new_heads[1],
        new_in_second, new_out_second, new_conv[2], new_gin[2], new_ggate[2], new_heads[2],
    )


def solution(mesh):
    rows = P(("rep", "shard"), None)
    both = P(("rep", "shard"))
    weights = (P("shard", None), P("shard", None), P(None, "shard"), P("shard"), P("shard"), P())
    reps, shards = mesh.shape["rep"], mesh.shape["shard"]

    def body(*arrays):
        return run(reps, shards, *arrays)

    return jax.shard_map(
        body,
        mesh=mesh,
        in_specs=(rows, rows, both, both) + weights * 3,
        out_specs=(rows, rows) + weights * 4,
        check_vma=False,
    )
```

```python
import functools

import jax
import jax.numpy as jnp
from jax import lax
from jax.experimental import pallas as pl
from jax.experimental.pallas import tpu as pltpu
from jax.sharding import PartitionSpec as P


STEP = 3
norm_eps = 1e-05
beta_first = 0.9
beta_second = 0.95
adam_eps = 1e-08
weight_decay = 0.1
matrix_rate = 0.005
vector_rate = 0.05
highest = lax.Precision.HIGHEST
f32 = jnp.float32
bf16 = jnp.bfloat16
LANES = 128


def dot(a, b, contract, precision=None):
    return lax.dot_general(
        a, b, (((contract[0],), (contract[1],)), ((), ())),
        preferred_element_type=f32, precision=precision,
    )


def rep_swap(x, bit, reps):
    return lax.ppermute(x, "rep", [(i, i ^ bit) for i in range(reps)])


def rep_bits(reps):
    return [1 << k for k in reversed(range(reps.bit_length() - 1))]


def rep_gather(x, reps):
    have = {0: x}
    for bit in rep_bits(reps):
        have.update({j | bit: rep_swap(v, bit, reps) for j, v in list(have.items())})
    return [have[j] for j in range(reps)]


def rep_scatter_sum(blocks, reps, wire):
    have = {j: b for j, b in enumerate(blocks)}
    for bit in reversed(rep_bits(reps)):
        keep = [j for j in have if not j & bit]
        have = {j: have[j].astype(f32) + rep_swap(have[j | bit].astype(wire), bit, reps).astype(f32) for j in keep}
    return have[0]


DEPTH = 4


def lined(shards):
    return shards == 2 * DEPTH


def over_z(moves):
    return [(2 * a + y, 2 * b + y) for a, b in moves for y in range(2)]


UP = over_z([(0, 1), (1, 2), (2, 3)])
DOWN = over_z([(3, 2), (2, 1), (1, 0)])
OUTWARD = over_z([(2, 3), (1, 0)])
RING = {j: over_z([(z, (z + j) % 4) for z in range(4)]) for j in (1, 2, 3)}


def across(zs):
    return [(2 * z + y, 2 * z + 1 - y) for z in zs for y in range(2)]


def gather_shards(block):
    me = lax.axis_index("shard")
    z, y = me // 2, me % 2
    far_own = lax.ppermute(block, "shard", across(range(4)))
    up = lax.ppermute(block, "shard", UP)
    down = lax.ppermute(block, "shard", DOWN)
    far_up = lax.ppermute(up, "shard", across((1, 2, 3)))
    far_down = lax.ppermute(down, "shard", across((0, 1, 2)))
    upper = lax.ppermute(up, "shard", UP[2:])
    lower = lax.ppermute(down, "shard", DOWN[2:])
    two = jnp.where(z < 2, lower, upper)
    far_two = lax.ppermute(two, "shard", across(range(4)))
    third = lax.ppermute(two, "shard", OUTWARD)
    far_third = lax.ppermute(third, "shard", across((0, 3)))
    at_third = jnp.where(z == 0, 3, jnp.where(z == 3, 0, z))
    found = []
    for where, value, far in (
        ((z + 3) % 4, up, far_up),
        ((z + 1) % 4, down, far_down),
        ((z + 2) % 4, two, far_two),
        (at_third, third, far_third),
        (z, block, far_own),
    ):
        found += [(2 * where + y, value), (2 * where + 1 - y, far)]
    return found


def slots(found):
    return jnp.stack([jnp.asarray(i, jnp.int32) for i, _ in found]), [v for _, v in found]


def reduce_shards(parts, shards):
    if not lined(shards):
        return lax.psum_scatter(parts, "shard", scatter_dimension=0, tiled=True)[0].astype(f32)
    me = lax.axis_index("shard")
    z, y = me // 2, me % 2

    def block(values, j, side):
        return lax.dynamic_index_in_dim(values, 2 * ((z + j) % 4) + side, 0, keepdims=False)

    def far(js):
        value = jnp.stack([block(parts, j, 1 - y) for j in js])
        return lax.ppermute(value, "shard", across(range(4))).astype(f32)

    def ring(value, j):
        return lax.ppermute(value, "shard", RING[j]).astype(f32)

    middle, sides, here = far((2,)), far((1, 3)), far((0,))
    second = (block(parts, 2, y).astype(f32) + middle[0]).astype(bf16)
    parts, second = lax.optimization_barrier((parts, second))
    two = ring(second, 2)
    one = ring((block(parts, 1, y).astype(f32) + sides[0]).astype(bf16), 1)
    three = ring((block(parts, 3, y).astype(f32) + sides[1]).astype(bf16), 3)
    return block(parts, 0, y).astype(f32) + here[0] + two + one + three


def sum_shards(x, shards):
    if shards & (shards - 1):
        return lax.psum(x, "shard")
    for bit in (1 << k for k in range(shards.bit_length() - 1)):
        x = x + lax.ppermute(x, "shard", [(i, i ^ bit) for i in range(shards)])
    return x


def softplus(v):
    return jnp.maximum(v, 0.0) + jnp.log1p(jnp.exp(-jnp.abs(v)))


def sigmoid(v):
    return 1.0 / (1.0 + jnp.exp(-v))


def iota(shape, axis):
    return lax.broadcasted_iota(jnp.int32, shape, axis)


PIECE = 2 * LANES


def sequences(row_ref, taps):
    span = row_ref.shape[1]
    number = jnp.broadcast_to(row_ref[0:1, :], (LANES, span)).T
    number = jnp.concatenate([number] * (PIECE // LANES), axis=1)
    row = iota(number.shape, 0)
    same = [((pltpu.roll(number, k, 0) == number) & (row >= k)).astype(f32) for k in range(1, taps)]
    return number, [None] + same


def conv_piece(raw, same, conv_ref, lanes, taps):
    total = conv_ref[taps : taps + 1, lanes] + conv_ref[0:1, lanes] * raw
    for k in range(1, taps):
        total = total + conv_ref[k : k + 1, lanes] * (same[k] * pltpu.roll(raw, k, 0))
    return total


def rates(raw, heads_ref):
    span = raw.shape[0]
    pre = raw + heads_ref[1:2, :]
    step = softplus(pre)
    log_decay = step * heads_ref[0:1, :]
    lower = (iota((span, span), 0) >= iota((span, span), 1)).astype(f32)
    running = dot(lower, log_decay, (1, 0), highest)
    return pre, step, log_decay, running, running.T


def spread(columns, first, count, head_size):
    lane = iota((columns.shape[0], LANES), 1) // head_size
    value = jnp.broadcast_to(columns[:, first : first + 1], lane.shape)
    for k in range(1, count):
        value = jnp.where(lane == k, columns[:, first + k : first + k + 1], value)
    return value


def prepare_kernel(me_ref, in_ref, out_ref, gain_in_ref, gain_out_ref, a_ref, b_ref, send_ref, *, dims, chunks, reps):
    hc, state, hr = dims
    inner = hc * reps
    piece = hc // chunks

    def scaled(values, gain):
        return (values.astype(bf16).astype(f32) * gain).astype(bf16)

    gain = gain_in_ref[...]
    rows = gain.shape[0]

    def columns(first, whole, own, t):
        parts = [in_ref[:, first + k * whole + t * own : first + k * whole + (t + 1) * own] for k in range(chunks)]
        return jnp.concatenate(parts, axis=1)

    for t in range(reps):

        @pl.when(me_ref[0] == t)
        def _(t=t):
            b_ref[:rows, :] = scaled(columns(0, inner // chunks, piece, t), gain)
            a_ref[:, :hc] = scaled(columns(inner, inner // chunks, piece, t), gain)
            step = columns(2 * inner + 2 * state, hr * reps // chunks, hr // chunks, t)
            step = jnp.concatenate([step, jnp.zeros((rows, LANES - hr), f32)], axis=1)
            a_ref[:, hc + 2 * state :] = scaled(step, gain)

    a_ref[:, hc : hc + 2 * state] = scaled(in_ref[:, 2 * inner : 2 * inner + 2 * state], gain)
    count = send_ref.shape[0]
    for k, first in enumerate((me_ref[1], me_ref[2])):
        first = pl.multiple_of(first, 8)
        block = scaled(out_ref[pl.ds(first, count), :], gain_out_ref[pl.ds(first, count), :])
        if k:
            send_ref[...] = block
        else:
            for q in range(block.shape[1] // hc):
                b_ref[rows + q * count : rows + (q + 1) * count, :] = block[:, q * hc : (q + 1) * hc]


def forward_kernel(at_ref, *refs, dims, count):
    hc, state, hs, taps = dims
    found, refs = refs[:count], refs[count:]
    u_ref, conv_ref, heads_ref, skip_ref, row_ref, p_ref, y_ref, w_ref, act_ref = refs

    @pl.when(pl.program_id(0) == 0)
    def _():
        for k, ref in enumerate(found):
            rows = ref.shape[0]
            w_ref[pl.ds(pl.multiple_of(at_ref[k] * rows, rows), rows), :] = ref[...]

    span = u_ref.shape[0]
    wide = hc + 2 * state
    p_ref[...] = jnp.dot(u_ref[...], w_ref[...], preferred_element_type=f32)
    number, same = sequences(row_ref, taps)
    for c in range(0, wide, PIECE):
        lanes = pl.ds(c, PIECE)
        conv = conv_piece(p_ref[:, lanes], same, conv_ref, lanes, taps)
        act_ref[:, lanes] = conv * sigmoid(conv)
    _, step, _, running, running_t = rates(p_ref[:, wide : wide + LANES], heads_ref)
    gram = dot(act_ref[:, hc + state : wide], act_ref[:, hc : hc + state], (1, 1), highest)
    causal = (number[:, 0:1] == row_ref[0:1, :]) & (iota((span, span), 0) >= iota((span, span), 1))
    per = LANES // hs
    lane = iota((span, LANES), 1) // hs
    for tile in range(hc // LANES):
        lanes = pl.ds(tile * LANES, LANES)
        x = act_ref[:, lanes]
        scaled = (x * spread(step, tile * per, per, hs)).astype(bf16)
        y = skip_ref[0:1, lanes] * x
        for k in range(per):
            h = tile * per + k
            decay = jnp.where(causal, jnp.exp(running[:, h : h + 1] - running_t[h : h + 1, :]), 0.0)
            mixing = (gram * decay).astype(bf16)
            y = y + dot(mixing, jnp.where(lane == k, scaled, jnp.zeros_like(scaled)), (1, 0))
        y_ref[:, lanes] = y


def gate_kernel(at_ref, *refs, count):
    found, refs = refs[:count], refs[count:]
    u_ref, cot_ref, y_ref, gate_ref, back_ref, sums_ref, wg_ref, wo_ref = refs
    width, hc = wg_ref.shape
    chunks = width // hc

    @pl.when(pl.program_id(0) == 0)
    def _():
        for k, ref in enumerate(found):
            per = ref.shape[0] * hc // (width + chunks * hc)
            rows = ref.shape[0] - chunks * per
            wg_ref[pl.ds(pl.multiple_of(at_ref[k] * rows, rows), rows), :] = ref[:rows, :]
            for q in range(chunks):
                at = pl.ds(pl.multiple_of(at_ref[k] * per, per), per)
                wo_ref[at, q * hc : (q + 1) * hc] = ref[rows + q * per : rows + (q + 1) * per, :]

    gate = jnp.dot(u_ref[...], wg_ref[...], preferred_element_type=f32)
    back = dot(cot_ref[...], wo_ref[...], (1, 1))
    gated = y_ref[...] * (gate * sigmoid(gate))
    ones = jnp.ones((8, gated.shape[1]), f32)
    gate_ref[...] = gate
    back_ref[...] = back
    sums_ref[0:8, :] = dot(ones, gated * gated, (1, 1), highest)
    sums_ref[8:16, :] = dot(ones, gated * back, (1, 1), highest)


def norm_kernel(y_ref, gate_ref, back_ref, sums_ref, mix_ref, dgate_ref, dy_ref, *, width):
    span = y_ref.shape[0]
    eye = (iota((span, span), 0) == iota((span, span), 1)).astype(f32)
    columns = dot(eye, sums_ref[...], (1, 1), highest)
    scale = lax.rsqrt(columns[:, 0:1] / width + norm_eps)
    pull = scale * scale * scale * (columns[:, 8:9] / width)
    y = y_ref[...]
    gate = gate_ref[...]
    sig = sigmoid(gate)
    gated = y * (gate * sig)
    mix_ref[...] = (gated * scale).astype(bf16)
    grad = scale * back_ref[...] - pull * gated
    dy_ref[...] = (grad * (gate * sig)).astype(bf16)
    dgate_ref[...] = (grad * y * (sig * (1.0 + gate * (1.0 - sig)))).astype(bf16)


def backward_kernel(
    p_ref, y_ref, dy_ref, conv_ref, heads_ref, skip_ref, row_ref,
    dp_ref, dconv_ref, dheads_ref, dskip_ref, act_ref, slope_ref, dact_ref, *, dims,
):
    hc, state, hs, taps = dims
    span = p_ref.shape[0]
    wide = hc + 2 * state

    @pl.when(pl.program_id(0) == 0)
    def _():
        dconv_ref[...] = jnp.zeros_like(dconv_ref)
        dheads_ref[...] = jnp.zeros_like(dheads_ref)
        dskip_ref[...] = jnp.zeros_like(dskip_ref)

    number, same = sequences(row_ref, taps)
    for c in range(0, wide, PIECE):
        lanes = pl.ds(c, PIECE)
        conv = conv_piece(p_ref[:, lanes], same, conv_ref, lanes, taps)
        sig = sigmoid(conv)
        act_ref[:, lanes] = conv * sig
        slope_ref[:, lanes] = sig * (1.0 + conv * (1.0 - sig))
    pre, step, log_decay, running, running_t = rates(p_ref[:, wide : wide + LANES], heads_ref)
    bmat = act_ref[:, hc : hc + state]
    cmat = act_ref[:, hc + state : wide]
    gram_t = dot(bmat, cmat, (1, 1), highest)
    causal_t = (number[:, 0:1] == row_ref[0:1, :]) & (iota((span, span), 0) <= iota((span, span), 1))
    per = LANES // hs
    lane = iota((span, LANES), 1) // hs
    dgram_t = jnp.zeros((span, span), f32)
    drun = jnp.zeros((span, LANES), f32)
    dstep = jnp.zeros((span, LANES), f32)
    for tile in range(hc // LANES):
        lanes = pl.ds(tile * LANES, LANES)
        x = act_ref[:, lanes]
        spread_step = spread(step, tile * per, per, hs)
        scaled = (x * spread_step).astype(bf16)
        dy = dy_ref[:, lanes]
        dscaled = jnp.zeros((span, LANES), f32)
        for k in range(per):
            h = tile * per + k
            decay_t = jnp.where(causal_t, jnp.exp(running_t[h : h + 1, :] - running[:, h : h + 1]), 0.0)
            mixing_t = (gram_t * decay_t).astype(bf16)
            own = lane == k
            dmix_t = dot(jnp.where(own, scaled, jnp.zeros_like(scaled)), dy, (1, 1))
            dgram_t = dgram_t + dmix_t * decay_t
            dscaled = dscaled + dot(mixing_t, jnp.where(own, dy, jnp.zeros_like(dy)), (1, 0))
        dy = dy.astype(f32)
        skip = skip_ref[0:1, lanes]
        to_head = (iota((LANES, LANES), 0) // hs + tile * per == iota((LANES, LANES), 1)).astype(f32)
        drun = drun + dot(dy * (y_ref[:, lanes] - skip * x) - scaled.astype(f32) * dscaled, to_head, (1, 0), highest)
        dstep = dstep + dot(dscaled * x, to_head, (1, 0), highest)
        dskip_ref[0:1, lanes] += jnp.sum(dy * x, axis=0, keepdims=True)
        dact_ref[:, lanes] = dscaled * spread_step + skip * dy
    half = dgram_t.astype(bf16)
    dact_ref[:, hc : hc + state] = dot(half, cmat.astype(bf16), (1, 0))
    dact_ref[:, hc + state : wide] = dot(half, bmat.astype(bf16), (0, 0))
    upper = (iota((span, span), 0) <= iota((span, span), 1)).astype(f32)
    dlog = dot(upper, drun, (1, 0), highest)
    draw = (dstep + dlog * heads_ref[0:1, :]) * sigmoid(pre)
    dheads_ref[0:1, :] += jnp.sum(dlog * log_decay, axis=0, keepdims=True)
    dheads_ref[1:2, :] += jnp.sum(draw, axis=0, keepdims=True)
    dp_ref[:, wide : wide + LANES] = draw.astype(bf16)
    for c in range(0, wide, PIECE):
        lanes = pl.ds(c, PIECE)
        raw = p_ref[:, lanes]
        grad = dact_ref[:, lanes] * slope_ref[:, lanes]
        back = conv_ref[0:1, lanes] * grad
        dconv_ref[0:1, lanes] += jnp.sum(grad * raw, axis=0, keepdims=True)
        dconv_ref[taps : taps + 1, lanes] += jnp.sum(grad, axis=0, keepdims=True)
        for k in range(1, taps):
            masked = same[k] * grad
            back = back + conv_ref[k : k + 1, lanes] * pltpu.roll(masked, span - k, 0)
            dconv_ref[k : k + 1, lanes] += jnp.sum(masked * pltpu.roll(raw, k, 0), axis=0, keepdims=True)
        dp_ref[:, lanes] = back.astype(bf16)


def grad_b_kernel(u_ref, dgate_ref, mix_ref, cot_ref, out_ref):
    count, rows, hc = out_ref.shape
    gate = dot(u_ref[...], dgate_ref[...], (0, 0)).astype(bf16)
    dl = gate.shape[0] // count
    out_ref[:, :dl, :] = gate.reshape(count, dl, hc)
    outer = dot(mix_ref[...], cot_ref[...], (0, 0)).astype(bf16)
    piece = outer.shape[0] // count
    for k in range((rows - dl) // piece):
        out_ref[:, dl + k * piece : dl + (k + 1) * piece, :] = outer[:, k * hc : (k + 1) * hc].reshape(count, piece, hc)


def branch_kernel(mix_ref, wo_ref, out_ref):
    out_ref[...] = jnp.dot(mix_ref[...], wo_ref[...], preferred_element_type=f32).astype(bf16)


def du_kernel(dgate_ref, wg_ref, dp_ref, wx_ref, out_ref):
    out_ref[...] = (dot(dgate_ref[...], wg_ref[...], (1, 1)) + dot(dp_ref[...], wx_ref[...], (1, 1))).astype(bf16)


def adam_update(weight, first, second, gradient, rate):
    first_new = beta_first * first + (1.0 - beta_first) * gradient
    second_new = beta_second * second + (1.0 - beta_second) * gradient * gradient
    first_hat = first_new * (1.0 / (1.0 - beta_first**STEP))
    second_hat = second_new * (1.0 / (1.0 - beta_second**STEP))
    weight_new = weight - rate * (first_hat / (jnp.sqrt(second_hat) + adam_eps) + weight_decay * weight)
    return (weight_new, first_new, second_new)


def adam_step(raw, gain_ref, w_ref, f_ref, s_ref, g_out, w_out, f_out, s_out):
    w = w_ref[...]
    grad = gain_ref[...] * raw
    g_out[...] = grad
    w_out[...], f_out[...], s_out[...] = adam_update(w, f_ref[...], s_ref[...], grad, matrix_rate)
    return w.astype(bf16).astype(f32) * raw


def dealt(a_ref, raw_ref, me_ref, i, chunks):
    reps = a_ref.shape[0]
    own = raw_ref.shape[1] // reps
    for z in range(chunks):

        @pl.when(i == z)
        def _(z=z):
            parts = [a_ref[t ^ me_ref[0], :, z * own : (z + 1) * own].astype(f32) for t in range(reps)]
            raw_ref[...] = jnp.concatenate(parts, axis=1)


def adam_gate_kernel(
    me_ref, a_ref, gain_ref, w_ref, f_ref, s_ref, g_out, w_out, f_out, s_out, gain_out, raw_ref, *, chunks
):
    @pl.when(pl.program_id(0) == 0)
    def _():
        gain_out[...] = jnp.zeros_like(gain_out)

    dealt(a_ref, raw_ref, me_ref, pl.program_id(0), chunks)
    product = adam_step(raw_ref[...], gain_ref, w_ref, f_ref, s_ref, g_out, w_out, f_out, s_out)
    gain_out[...] += jnp.sum(product, axis=1, keepdims=True)


def adam_rest_kernel(
    me_ref, a_ref, part_ref, gain_ref, w_ref, f_ref, s_ref, g_in, w_in, f_in, s_in,
    g_out, w_out, f_out, s_out, gain_out, raw_ref, *, chunks, dims, start, width,
):
    hc, state, hr = dims
    reps = a_ref.shape[0]
    wide = hc + 2 * state
    i = pl.program_id(0)

    @pl.when(i == 0)
    def _():
        gain_out[...] = part_ref[...]

    dealt(a_ref, raw_ref, me_ref, i, chunks)

    @pl.when(i == pl.num_programs(0) - 1)
    def _():
        shared = a_ref[0, :, hc:wide].astype(f32)
        for t in range(1, reps):
            shared = shared + a_ref[t, :, hc:wide].astype(f32)
        raw_ref[:, : 2 * state] = shared
        own = hr // chunks
        row, column = iota((LANES, LANES), 0), iota((LANES, LANES), 1)
        steps = jnp.zeros((a_ref.shape[1], LANES), f32)
        for t in range(reps):
            there = (row < hr) & (column == (row // own) * own * reps + t * own + row % own)
            steps = steps + dot(a_ref[t ^ me_ref[0], :, wide:], there.astype(bf16), (1, 0))
        raw_ref[:, 2 * state : 2 * state + LANES] = steps
        raw_ref[:, 2 * state + LANES :] = jnp.zeros_like(raw_ref[:, 2 * state + LANES :])

    product = adam_step(raw_ref[...], gain_ref, w_ref, f_ref, s_ref, g_out, w_out, f_out, s_out)
    inside = iota(product.shape, 1) + (i + start) * product.shape[1] < width
    gain_out[...] += jnp.sum(jnp.where(inside, product, 0.0), axis=1, keepdims=True)


def adam_out_kernel(me_ref, a_ref, gain_ref, w_ref, f_ref, s_ref, g_out, w_out, f_out, s_out, gain_out):
    product = adam_step(a_ref[0].astype(f32), gain_ref, w_ref, f_ref, s_ref, g_out, w_out, f_out, s_out)
    gain_out[...] = jnp.sum(product, axis=1, keepdims=True)


def cost(flops, nbytes, transcendentals=0):
    return pl.CostEstimate(flops=flops, bytes_accessed=nbytes, transcendentals=transcendentals)


def shape(dims, dtype=f32):
    return jax.ShapeDtypeStruct(dims, dtype)


def kernel(body, **settings):
    return pl.pallas_call(body, **settings)


def rows_spec(span, width):
    return pl.BlockSpec((span, width), lambda g: (g, 0))


def whole_spec(dims):
    return pl.BlockSpec(dims, lambda g: (0,) * len(dims))


def run(
    reps, shards,
    tokens, cotangent, segment, live_rows,
    in_weight, out_weight, conv_table, norm_in, norm_gate, head_params,
    in_first, out_first, conv_first, norm_in_first, norm_gate_first, heads_first,
    in_second, out_second, conv_second, norm_in_second, norm_gate_second, heads_second,
):
    own_rows, width = tokens.shape
    span = own_rows // live_rows.shape[0]
    rows = own_rows * reps
    groups = rows // span
    inner = norm_gate.shape[0] * shards
    taps = conv_table.shape[0] - 1
    piece = conv_table.shape[1]
    channels = piece * shards
    heads = head_params.shape[1]
    hs = inner // heads
    state = (channels - inner) // 2
    hr = heads // reps
    hc = inner // reps
    wide = hc + 2 * state
    dl = in_weight.shape[0]
    projections = in_weight.shape[1]
    rep = lax.axis_index("rep")
    me = lax.axis_index("shard")
    dims = (hc, state, hs, taps)

    chunks = DEPTH if lined(shards) and reps == 4 else 1
    index = rep.astype(jnp.int32)

    def own_part(values):
        whole = values.shape[-1] // chunks
        values = values.reshape(*values.shape[:-1], chunks, whole)
        starts = [0] * (values.ndim - 1) + [rep * (whole // reps)]
        values = lax.dynamic_slice(values, starts, (*values.shape[:-1], whole // reps))
        return values.reshape(*values.shape[:-2], chunks * (whole // reps))

    def in_place(values, all_of):
        whole = all_of // chunks
        values = values.reshape(*values.shape[:-1], chunks, whole // reps)
        full = jnp.zeros((*values.shape[:-1], whole), f32)
        full = lax.dynamic_update_slice(full, values, [0] * (values.ndim - 1) + [rep * (whole // reps)])
        return full.reshape(*full.shape[:-2], all_of)

    gain_in = norm_in.astype(bf16).astype(f32)[:, None]
    gain_gate = norm_gate.astype(bf16).astype(f32)[:, None]
    out_rows = out_weight.shape[0] // reps
    halves = width // hc
    if chunks > 1:
        row = me % 2
        side, core = rep // 2, rep % 2
        keep = (2 * core + row) * out_rows
        send = (2 * core + 1 - row) * out_rows
        deal = [(r * shards + 2 * z + r // 2, r * shards + 2 * z + 1 - r // 2) for r in range(reps) for z in range(DEPTH)]
    else:
        keep = send = out_rows * rep
        deal = [(r * shards + s, s * reps + r) for r in range(reps) for s in range(shards)]
    back = [(b, a) for a, b in deal]
    wx_own, wb_own, wo_send = kernel(
        functools.partial(prepare_kernel, dims=(hc, state, hr), chunks=chunks, reps=reps),
        grid_spec=pltpu.PrefetchScalarGridSpec(
            num_scalar_prefetch=1,
            grid=(1,),
            in_specs=[
                pl.BlockSpec(v, lambda i, m: (0, 0)) for v in (in_weight.shape, out_weight.shape, (dl, 1), gain_gate.shape)
            ],
            out_specs=[
                pl.BlockSpec(v, lambda i, m: (0, 0))
                for v in ((dl, wide + LANES), (dl + out_rows * halves, hc), (out_rows, width))
            ],
        ),
        out_shape=[
            shape((dl, wide + LANES), bf16), shape((dl + out_rows * halves, hc), bf16), shape((out_rows, width), bf16)
        ],
        cost_estimate=cost(4 * dl * wide, 12 << 20),
    )(jnp.stack([index, keep.astype(jnp.int32), send.astype(jnp.int32)]), in_weight, out_weight, gain_in, gain_gate)

    live = (jnp.arange(own_rows) % span < jnp.repeat(live_rows, span))[:, None]
    values = jnp.where(live, tokens.astype(f32), 0.0)
    scale_in = lax.rsqrt(jnp.mean(values * values, axis=1, keepdims=True) + norm_eps)
    u_own = (values * scale_in).astype(bf16)
    cot_own = jnp.where(live, cotangent, jnp.zeros_like(cotangent))
    numbers = jnp.pad(segment.astype(bf16)[None], ((0, 7), (0, width - own_rows)))
    blocks = rep_gather(jnp.concatenate([u_own, numbers], axis=0), reps)
    u = jnp.concatenate([v[:own_rows] for v in blocks])
    row_numbers = jnp.concatenate([v[own_rows:, :own_rows] for v in blocks], axis=1).astype(f32)
    row_numbers = jnp.broadcast_to(row_numbers[0:1], (8, rows))
    cot = jnp.concatenate(rep_gather(cot_own, reps))

    conv_all = lax.dynamic_update_slice(
        jnp.zeros((8, channels), f32),
        jnp.pad(conv_table.astype(bf16).astype(f32), ((0, 7 - taps), (0, 0))),
        (0, piece * me),
    )
    conv_all = sum_shards(conv_all, shards)
    conv = jnp.concatenate([own_part(conv_all[:, :inner]), conv_all[:, inner:]], axis=1)
    own_heads = own_part(head_params)
    head_rows = jnp.pad(jnp.stack([-jnp.exp(own_heads[0]), own_heads[2]]), ((0, 6), (0, LANES - hr)))
    skip = jnp.broadcast_to(jnp.repeat(own_heads[1], hs)[None], (8, hc))

    got = lax.ppermute(wo_send, ("rep", "shard"), deal)
    got = jnp.concatenate([got[:, k * hc : (k + 1) * hc] for k in range(halves)], axis=0)
    if chunks > 1:
        got = jnp.where(side == row, wb_own[dl:], got)
    wb_own = jnp.concatenate([wb_own[:dl], got], axis=0)
    if lined(shards):
        at_a, found_a = slots(gather_shards(wx_own))
        at_b, found_b = slots(gather_shards(wb_own))
    else:
        at_a = at_b = jnp.zeros((1,), jnp.int32)
        found_a = [lax.all_gather(wx_own, "shard", axis=0, tiled=True)]
        every = lax.all_gather(wb_own, "shard", axis=0, tiled=False)
        edges = [0, dl] + [dl + (k + 1) * out_rows for k in range(halves)]
        found_b = [jnp.concatenate([every[:, a:b].reshape(-1, hc) for a, b in zip(edges, edges[1:])], axis=0)]

    def fixed(dims):
        return pl.BlockSpec(dims, lambda g, at: (0,) * len(dims))

    def by_group(columns):
        return pl.BlockSpec((span, columns), lambda g, at: (g, 0))

    def along_rows(count):
        return pl.BlockSpec((count, span), lambda g, at: (0, g))

    p, y, wx = kernel(
        functools.partial(forward_kernel, dims=dims, count=len(found_a)),
        grid_spec=pltpu.PrefetchScalarGridSpec(
            num_scalar_prefetch=1,
            grid=(groups,),
            in_specs=[fixed(v.shape) for v in found_a]
            + [by_group(width), fixed(conv.shape), fixed(head_rows.shape), fixed(skip.shape), along_rows(8)],
            out_specs=[by_group(wide + LANES), by_group(hc), fixed((width, wide + LANES))],
            scratch_shapes=[pltpu.VMEM((span, wide), f32)],
        ),
        out_shape=[shape((rows, wide + LANES)), shape((rows, hc)), shape((width, wide + LANES), bf16)],
        cost_estimate=cost(2 * rows * width * (wide + LANES), 16 << 20, rows * span * hr),
    )(at_a, *found_a, u, conv, head_rows, skip, row_numbers)

    gate, grad_mix, sums, wg, wo = kernel(
        functools.partial(gate_kernel, count=len(found_b)),
        grid_spec=pltpu.PrefetchScalarGridSpec(
            num_scalar_prefetch=1,
            grid=(groups,),
            in_specs=[fixed(v.shape) for v in found_b] + [by_group(width), by_group(width), by_group(hc)],
            out_specs=[by_group(hc), by_group(hc), along_rows(16), fixed((width, hc)), fixed((hc, width))],
        ),
        out_shape=[
            shape((rows, hc)), shape((rows, hc)), shape((16, rows)), shape((width, hc), bf16), shape((hc, width), bf16)
        ],
        cost_estimate=cost(4 * rows * width * hc, 24 << 20, rows * hc),
    )(at_b, *found_b, u, cot, y)
    for bit in rep_bits(reps):
        there = rep_swap(sums, bit, reps)
        order = [there[:, (j ^ bit) * own_rows : ((j ^ bit) + 1) * own_rows] for j in range(reps)]
        sums = sums + jnp.concatenate(order, axis=1)

    mix, dgate, dy = kernel(
        functools.partial(norm_kernel, width=inner),
        grid=(groups,),
        in_specs=[rows_spec(span, hc)] * 3 + [pl.BlockSpec((16, span), lambda g: (0, g))],
        out_specs=[rows_spec(span, hc)] * 3,
        out_shape=[shape((rows, hc), bf16)] * 3,
        cost_estimate=cost(20 * rows * hc, 15 << 20, rows * hc),
    )(y, gate, grad_mix, sums)

    half = shards // 2
    per = out_rows
    rows_b = dl + per * halves
    part_b = kernel(
        grad_b_kernel,
        grid=(2,),
        in_specs=[
            pl.BlockSpec((rows, width // 2), lambda i: (0, i)), whole_spec((rows, hc)),
            pl.BlockSpec((rows, hc // 2), lambda i: (0, i)), whole_spec((rows, width)),
        ],
        out_specs=pl.BlockSpec((half, rows_b, hc), lambda i: (i, 0, 0)),
        out_shape=shape((shards, rows_b, hc), bf16),
        cost_estimate=cost(4 * rows * width * hc, 15 << 20),
    )(u, dgate, mix, cot)
    sum_b = reduce_shards(part_b, shards).astype(bf16)
    b_sums = jnp.stack(rep_gather(sum_b[:dl], reps))
    own_out = jnp.concatenate([sum_b[dl + k * per : dl + (k + 1) * per] for k in range(halves)], axis=1)
    other_out = lax.ppermute(own_out, ("rep", "shard"), back)
    if chunks > 1:
        own_out = jnp.concatenate([jnp.where(row == 0, own_out, other_out), jnp.where(row == 0, other_out, own_out)])
        over = lax.ppermute(
            own_out, ("rep", "shard"),
            [(r * shards + 2 * z + r // 2, (r ^ 2) * shards + 2 * z + r // 2) for r in range(reps) for z in range(DEPTH)],
        )
        own_out = jnp.where(side == row, own_out, over)
        out_sums = jnp.stack([own_out, rep_swap(own_out, 1, reps)])
    else:
        out_sums = jnp.stack(rep_gather(other_out, reps))
    branch = kernel(
        branch_kernel,
        grid=(groups,),
        in_specs=[rows_spec(span, hc), whole_spec(wo.shape)],
        out_specs=rows_spec(span, width),
        out_shape=shape((rows, width), bf16),
        cost_estimate=cost(2 * rows * width * hc, 8 << 20),
    )(mix, wo).reshape(reps, own_rows, width)
    branch_sum = rep_scatter_sum([branch[j] for j in range(reps)], reps, bf16)
    block_out = (values + branch_sum).astype(bf16)

    dp, dconv, dheads, dskip = kernel(
        functools.partial(backward_kernel, dims=dims),
        grid=(groups,),
        in_specs=[
            rows_spec(span, wide + LANES), rows_spec(span, hc), rows_spec(span, hc), whole_spec(conv.shape),
            whole_spec(head_rows.shape), whole_spec(skip.shape), pl.BlockSpec((8, span), lambda g: (0, g)),
        ],
        out_specs=[
            rows_spec(span, wide + LANES), whole_spec(conv.shape), whole_spec(head_rows.shape),
            whole_spec(skip.shape),
        ],
        out_shape=[shape((rows, wide + LANES), bf16), shape(conv.shape), shape(head_rows.shape), shape(skip.shape)],
        scratch_shapes=[pltpu.VMEM((span, wide), f32)] * 3,
        cost_estimate=cost(4 * rows * span * hc * 2, 12 << 20, rows * span * hr),
    )(p, y, dy, conv, head_rows, skip, row_numbers)

    head_part = jnp.stack([dheads[0, :hr], jnp.sum(dskip[0].reshape(hr, hs), axis=1), dheads[1, :hr]])
    small = jnp.concatenate(
        [
            in_place(dconv[:, :hc], inner),
            dconv[:, hc:],
            jnp.pad(in_place(head_part, heads), ((0, 5), (0, LANES - heads))),
        ],
        axis=1,
    )
    for bit in reversed(rep_bits(reps)):
        small = small + rep_swap(small, bit, reps)
    small = sum_shards(small, shards)

    part_a = dot(u, dp, (0, 0)).astype(bf16)
    part_a = part_a.reshape(shards, dl, wide + LANES)
    x_sums = jnp.stack(rep_gather(reduce_shards(part_a, shards).astype(bf16), reps))
    du = kernel(
        du_kernel,
        grid=(groups,),
        in_specs=[
            rows_spec(span, hc), whole_spec(wg.shape), rows_spec(span, wide + LANES), whole_spec(wx.shape),
        ],
        out_specs=rows_spec(span, width),
        out_shape=shape((rows, width), bf16),
        cost_estimate=cost(2 * rows * width * (hc + wide + LANES), 12 << 20),
    )(dgate, wg, dp, wx).reshape(reps, own_rows, width)
    du = rep_scatter_sum([du[j] for j in range(reps)], reps, bf16)
    scaled = values * scale_in
    pulled = scale_in * (du - scaled * jnp.mean(du * scaled, axis=1, keepdims=True))
    input_grad = jnp.where(live, (cot_own.astype(f32) + pulled).astype(bf16), jnp.zeros_like(cot_own))

    tile = inner // chunks if chunks > 1 else hc
    tiles = inner // tile
    kept = (hc, state, hr)

    def columns(start):
        return pl.BlockSpec((dl, tile), lambda i, m: (0, i + start))

    def steady(dims):
        return pl.BlockSpec(dims, lambda i, m: (0,) * len(dims))

    in_shapes = [shape(in_weight.shape)] * 4 + [shape((dl, 1))]
    scratch = [pltpu.VMEM((dl, tile), f32)]
    gate_done = kernel(
        functools.partial(adam_gate_kernel, chunks=tiles),
        grid_spec=pltpu.PrefetchScalarGridSpec(
            num_scalar_prefetch=1,
            grid=(tiles,),
            in_specs=[steady(b_sums.shape), steady((dl, 1))] + [columns(0)] * 3,
            out_specs=[columns(0)] * 4 + [steady((dl, 1))],
            scratch_shapes=scratch,
        ),
        out_shape=in_shapes,
        cost_estimate=cost(20 * dl * inner, 30 * dl * inner),
    )(index[None], b_sums, gain_in, in_weight, in_first, in_second)
    grad_in_weight, new_in, new_in_first, new_in_second, in_gain_grad = kernel(
        functools.partial(adam_rest_kernel, chunks=tiles, dims=kept, start=tiles, width=projections),
        grid_spec=pltpu.PrefetchScalarGridSpec(
            num_scalar_prefetch=1,
            grid=(pl.cdiv(projections, tile) - tiles,),
            in_specs=[steady(x_sums.shape), steady((dl, 1)), steady((dl, 1))]
            + [columns(tiles)] * 3
            + [pl.BlockSpec(memory_space=pl.ANY)] * 4,
            out_specs=[columns(tiles)] * 4 + [steady((dl, 1))],
            scratch_shapes=scratch,
        ),
        out_shape=in_shapes,
        input_output_aliases={7 + k: k for k in range(4)},
        cost_estimate=cost(20 * dl * inner, 30 * dl * inner),
    )(index[None], x_sums, gate_done[4], gain_in, in_weight, in_first, in_second, *gate_done[:4])

    shares, share_rows = out_sums.shape[:2]
    out_spec = pl.BlockSpec((share_rows, width), lambda i, m: (i, 0))
    out_column = pl.BlockSpec((share_rows, 1), lambda i, m: (i, 0))
    grad_out_weight, new_out, new_out_first, new_out_second, out_gain_grad = kernel(
        adam_out_kernel,
        grid_spec=pltpu.PrefetchScalarGridSpec(
            num_scalar_prefetch=1,
            grid=(shares,),
            in_specs=[
                pl.BlockSpec((1, share_rows, width), lambda i, m: (i ^ (m[0] % shares), 0, 0)), out_column,
            ]
            + [out_spec] * 3,
            out_specs=[out_spec] * 4 + [out_column],
        ),
        out_shape=[shape(out_weight.shape)] * 4 + [shape((out_weight.shape[0], 1))],
        cost_estimate=cost(20 * out_weight.size, 30 * out_weight.size),
    )(index[None], out_sums, gain_gate, out_weight, out_first, out_second)

    grad_conv = lax.dynamic_slice(small, (0, piece * me), (taps + 1, piece))
    grad_heads = small[:3, channels : channels + heads]
    grad_norm_in = in_gain_grad[:, 0]
    grad_norm_gate = out_gain_grad[:, 0]
    new_conv = adam_update(conv_table, conv_first, conv_second, grad_conv, vector_rate)
    new_gin = adam_update(norm_in, norm_in_first, norm_in_second, grad_norm_in, vector_rate)
    new_ggate = adam_update(norm_gate, norm_gate_first, norm_gate_second, grad_norm_gate, vector_rate)
    new_heads = adam_update(head_params, heads_first, heads_second, grad_heads, vector_rate)
    return (
        block_out, input_grad,
        grad_in_weight, grad_out_weight, grad_conv, grad_norm_in, grad_norm_gate, grad_heads,
        new_in, new_out, new_conv[0], new_gin[0], new_ggate[0], new_heads[0],
        new_in_first, new_out_first, new_conv[1], new_gin[1], new_ggate[1], new_heads[1],
        new_in_second, new_out_second, new_conv[2], new_gin[2], new_ggate[2], new_heads[2],
    )


def solution(mesh):
    rows = P(("rep", "shard"), None)
    both = P(("rep", "shard"))
    weights = (P("shard", None), P("shard", None), P(None, "shard"), P("shard"), P("shard"), P())
    reps, shards = mesh.shape["rep"], mesh.shape["shard"]

    def body(*arrays):
        return run(reps, shards, *arrays)

    return jax.shard_map(
        body,
        mesh=mesh,
        in_specs=(rows, rows, both, both) + weights * 3,
        out_specs=(rows, rows) + weights * 4,
        check_vma=False,
    )
```
